32 devices in a mesh: grp: 2 (over x), ctx: 16 (over z, y, core).
Axes of the slice: x: 2, y: 2, z: 4, core: 2. Of those that a mesh axis runs over, the one named last changes fastest.
Arguments:
- queries: bfloat16 [960, 4096], P(None, ('grp', 'ctx')), parts along dimension 1, may hold values from -6 to 6
- key_rows: bfloat16 [960, 4096], P(None, ('grp', 'ctx')), parts along dimension 1, may hold values from -6 to 6
- value_rows: bfloat16 [960, 4096], P(None, ('grp', 'ctx')), parts along dimension 1, may hold values from -6 to 6
- short_taps: float32 [3, 960, 7], replicated, may hold values from -2 to 2
- long_filter: bfloat16 [960, 2048], P('ctx'), may hold values from -0.125 to 0.125
Outputs:
- mixed: bfloat16 [960, 4096], P(None, ('grp', 'ctx')), parts along dimension 1
The draws below stay inside these ranges and needn't reach their ends.
There are 2 independent parts, one for each index of `grp`. The reference program is written for one: setup_inputs(seed, part) draws one part's arguments, and reference() takes and returns one part's arrays. A program takes and returns all parts, laid end to end along the dimension named above; an argument that names none is the same for every part. Nothing has to cross between parts.
All inputs are finite; a program needn't handle non-finite values.
Results may differ from the reference program's by a relative error of at most 0.0057.
Values may be sent and summed in bfloat16 or wider, within the bound.
A program may use at most 64 MiB of HBM per device.

```python
import jax
import jax.numpy as jnp

D = 960
TAPS = 7
SEQ = 2048


def block_scale(stream_key, shape, shards, least, top_value):
    loudness = 1.0
    for axis_at, parts in shards:
        steps = jax.random.uniform(jax.random.fold_in(jax.random.fold_in(stream_key, 6), axis_at), (parts,), jnp.float32, least / len(shards), top_value / len(shards))
        loudness = loudness * jnp.repeat(jnp.exp(steps), shape[axis_at] // parts).reshape((-1,) + (1,) * (len(shape) - 1 - axis_at))
    return loudness


def bell_draw(own_key, extent, scale, limit, split=(), dtype=jnp.bfloat16):
    drawn = scale * jax.random.normal(own_key, extent, jnp.float32)
    if split:
        drawn = drawn * block_scale(own_key, extent, split, -0.22, 0.18)
    return jnp.clip(drawn, -limit, limit).astype(dtype)


def setup_inputs(seed: int = 0, part: int = 0) -> dict:
    key_of = jax.random.split(jax.random.key(seed), 6)
    part_splits = jax.random.split(jax.random.fold_in(key_of[5], part), 6)
    queries = bell_draw(part_splits[0], (D, SEQ), 1.0, 6.0, ((1, 16),))
    key_rows = bell_draw(part_splits[1], (D, SEQ), 1.0, 6.0, ((1, 16),))
    value_rows = bell_draw(part_splits[2], (D, SEQ), 1.0, 6.0, ((1, 16),))
    short_taps = bell_draw(key_of[3], (3, D, TAPS), TAPS ** -0.5, 2.0, (), jnp.float32)
    long_filter = bell_draw(key_of[4], (D, SEQ), SEQ ** -0.5, 0.125, ((0, 16),))
    return dict(queries=queries, key_rows=key_rows, value_rows=value_rows, short_taps=short_taps, long_filter=long_filter)


def short_conv(rows, taps):
    length = rows.shape[1]
    padded = jnp.pad(rows.astype(jnp.float32), ((0, 0), (TAPS - 1, TAPS - 1)))
    mirrored = taps[::-1, :]
    causal = jnp.zeros(rows.shape, jnp.float32)
    anticausal = jnp.zeros(rows.shape, jnp.float32)
    for offset in range(TAPS):
        begin = TAPS - 1 - offset
        causal = causal + taps[:, offset, None] * padded[:, begin:begin + length]
        later = TAPS - 1 + offset
        anticausal = anticausal + mirrored[:, offset, None] * padded[:, later:later + length]
    return causal, anticausal


def reference(queries, key_rows, value_rows, short_taps, long_filter):
    query_fwd, query_bwd = short_conv(queries, short_taps[0])
    key_fwd, key_bwd = short_conv(key_rows, short_taps[1])
    value_fwd, value_bwd = short_conv(value_rows, short_taps[2])
    product_a = (key_fwd * value_fwd).astype(jnp.bfloat16)
    product_b = (key_bwd * value_bwd).astype(jnp.bfloat16)
    padded_len = 2 * SEQ
    filter_spec = jnp.fft.rfft(long_filter.astype(jnp.float32), n=padded_len, axis=1)
    spec_a = jnp.fft.rfft(product_a.astype(jnp.float32), n=padded_len, axis=1)
    mixed_a = jnp.fft.irfft(filter_spec * spec_a, n=padded_len, axis=1)[:, :SEQ]
    mixed_a = mixed_a.astype(jnp.float32).astype(jnp.bfloat16)
    spec_b = jnp.fft.rfft(product_b.astype(jnp.float32), n=padded_len, axis=1)
    mixed_b = jnp.fft.irfft(jnp.conj(filter_spec[::-1]) * spec_b, n=padded_len, axis=1)[:, :SEQ]
    mixed_b = mixed_b.astype(jnp.float32).astype(jnp.bfloat16)
    result = query_fwd * mixed_a.astype(jnp.float32) + query_bwd * mixed_b.astype(jnp.float32)
    return result.astype(jnp.bfloat16)
```

```python
import functools

import jax
import jax.numpy as jnp
import numpy as np
from jax import lax
from jax.experimental import pallas as pl
from jax.experimental.pallas import tpu as pltpu
from jax.sharding import PartitionSpec as P

TAPS = 7
LANES = 128
F32 = jnp.float32
BF16 = jnp.bfloat16


def dims_of(cblk):
    cpad = -(-cblk // 16) * 16
    low = (cpad - cblk) // 2
    rows = 16 if cpad % 16 == 0 and 2 * low + cblk == cpad else cpad
    return cpad, low, rows


def unit(flip):
    i = lax.broadcasted_iota(jnp.int32, (LANES, LANES), 0)
    j = lax.broadcasted_iota(jnp.int32, (LANES, LANES), 1)
    j = LANES - 1 - j if flip else j
    return (i == j).astype(F32).astype(BF16)


def dft_tables():
    t = np.arange(2 * LANES)[:, None]
    angle = np.pi * t * (np.arange(LANES)[None] + 0.5) / LANES
    fwd = np.concatenate([np.cos(angle), -np.sin(angle)], axis=1)
    inv = fwd[LANES:].T / LANES

    def pair(x):
        high = x.astype(BF16)
        return np.stack([high, (x - high.astype(np.float64)).astype(BF16)])

    return pair(fwd), pair(inv)


def mirror(cblk):
    cpad, low, _ = dims_of(cblk)
    i = lax.broadcasted_iota(jnp.int32, (LANES, LANES), 0)
    j = lax.broadcasted_iota(jnp.int32, (LANES, LANES), 1)
    blocks = i // cpad + j // cpad == LANES // cpad - 1
    return (blocks & (i % cpad + j % cpad == cblk - 1 + 2 * low)).astype(F32).astype(BF16)


def mm(a, b):
    return lax.dot_general(a, b, (((1,), (0,)), ((), ())), preferred_element_type=F32)


def to_time_major(mat, x):
    return lax.dot_general(mat, x, (((1,), (1,)), ((), ())), preferred_element_type=F32)


def to_channel_major(x, mat):
    return lax.dot_general(x, mat, (((0,), (0,)), ((), ())), preferred_element_type=F32)


def short_sum(xs, taps, way, which, lanes):
    total = None
    for j in range(TAPS):
        start = 8 - j if way == 0 else 8 + j
        term = taps[way, which, j : j + 1, lanes] * xs[which, start : start + LANES, lanes]
        total = term if total is None else total + term
    return total


def kernel(
    n, cblk, q_hbm, k_hbm, v_hbm, taps_hbm, filt_hbm, fwd_hbm, inv_hbm, out,
    xin, tin, filt, in_sem, alt, taps, xf, xs, qmix, snd, rcv, osnd, orcv, fwd, inv, hh, xh, yh,
    hs_sem, hr_sem, s_sem, r_sem, os_sem, or_sem,
):
    cpad, low, rows = dims_of(cblk)
    nch = cpad // rows
    cp = n * cpad
    me = lax.axis_index("ctx")
    groups = cp // LANES
    per = LANES // cpad

    barrier = pltpu.get_barrier_semaphore()

    def greet(o, carry):
        pl.semaphore_signal(barrier, inc=1, device_id={"ctx": lax.rem(me + o, n)})
        return carry

    lax.fori_loop(1, n, greet, 0)

    loads = [
        pltpu.make_async_copy(src, dst, in_sem.at[i])
        for i, (src, dst) in enumerate((
            (q_hbm, xin.at[0]), (k_hbm, xin.at[1]), (v_hbm, xin.at[2]),
            (taps_hbm, tin), (filt_hbm, filt), (fwd_hbm, fwd), (inv_hbm, inv),
        ))
    ]
    for i in (1, 2, 3, 0, 4, 5, 6):
        loads[i].start()

    eye = unit(False)
    flip = unit(True)
    turn_rows = mirror(cblk)
    channels = n * cblk
    held = 8 + channels
    taps[...] = jnp.zeros((2, 3, 8, cp), F32)
    alt[...] = jnp.zeros((3, 8, cp), F32)
    for a in range(3):
        xf[a, 0:8, :] = jnp.zeros((8, LANES), F32)
        xf[a, held : held + 16, :] = jnp.zeros((16, LANES), F32)

    def turn(a):
        loads[a].wait()
        xf[a, 8:held, :] = xin[a].astype(F32)
        for g in range(groups):
            starts = [8 + (g * per + s) * cblk - low for s in range(per)]
            wide = jnp.concatenate([xf[a, i : i + cpad, :] for i in starts], axis=0).astype(BF16)
            xs[a, 8 : 8 + LANES, g * LANES : (g + 1) * LANES] = to_time_major(eye, wide)

    def halo(a, up):
        if up:
            return pltpu.make_async_remote_copy(
                src_ref=xs.at[a, pl.ds(LANES, 8)], dst_ref=xs.at[a, pl.ds(0, 8)],
                send_sem=hs_sem.at[0, a], recv_sem=hr_sem.at[0, a],
                device_id={"ctx": lax.rem(me + 1, n)},
            )
        return pltpu.make_async_remote_copy(
            src_ref=xs.at[a, pl.ds(8, 8)], dst_ref=xs.at[a, pl.ds(8 + LANES, 8)],
            send_sem=hs_sem.at[1, a], recv_sem=hr_sem.at[1, a],
            device_id={"ctx": lax.rem(me + n - 1, n)},
        )

    @pl.when(me == 0)
    def _():
        xs[:, 0:8, :] = jnp.zeros((3, 8, cp), F32)

    @pl.when(me == n - 1)
    def _():
        xs[:, 8 + LANES : 16 + LANES, :] = jnp.zeros((3, 8, cp), F32)

    def halo_wait(arrays):
        @pl.when(me > 0)
        def _():
            for a in arrays:
                halo(a, True).wait_recv()

        @pl.when(me < n - 1)
        def _():
            for a in arrays:
                halo(a, False).wait_recv()

    def halo_start(arrays):
        @pl.when(me < n - 1)
        def _():
            for a in arrays:
                halo(a, True).start()

        @pl.when(me > 0)
        def _():
            for a in arrays:
                halo(a, False).start()

    turn(1)
    turn(2)
    pl.semaphore_wait(barrier, n - 1)
    halo_start((1, 2))
    turn(0)
    halo_start((0,))
    loads[3].wait()
    for ref, shift in ((taps.at[0], low), (alt, cpad - cblk - low)):
        for b in range(n):
            base = b * cblk - shift
            lo, hi = max(base, 0), min(base + cpad, channels)
            at = b * cpad + lo - base
            ref[:, 0:TAPS, at : at + hi - lo] = tin[:, :, lo:hi]
    turner = unit(True).astype(F32)
    for g in range(groups):
        source = alt[:, :, cp - (g + 1) * LANES : cp - g * LANES].reshape(24, LANES)
        taps[1, :, :, g * LANES : (g + 1) * LANES] = jnp.dot(
            source, turner, precision=lax.Precision.HIGHEST, preferred_element_type=F32
        ).reshape(3, 8, LANES)
    for i in (4, 5, 6):
        loads[i].wait()
    place = lax.broadcasted_iota(jnp.int32, (cpad, cblk), 0) - lax.broadcasted_iota(jnp.int32, (cpad, cblk), 1)
    place = (place == low).astype(F32).astype(BF16)
    hpad = mm(place, filt[...]).astype(BF16)
    lag = [jnp.zeros((cpad, LANES), BF16)] + [hpad[:, d * LANES : (d + 1) * LANES] for d in range(n)]
    for d in range(n):
        line = jnp.concatenate([lag[d], lag[d + 1]], axis=1)
        spec = mm(line, fwd[0]) + mm(line, fwd[1])
        hh[d] = spec

    halo_wait((1, 2))
    for g in range(groups):
        ls = slice(g * LANES, (g + 1) * LANES)
        pa = (short_sum(xs, taps, 0, 1, ls) * short_sum(xs, taps, 0, 2, ls)).astype(BF16)
        pb = (short_sum(xs, taps, 1, 1, ls) * short_sum(xs, taps, 1, 2, ls)).astype(BF16)
        pa = to_channel_major(pa, eye).astype(BF16)
        pb = mm(turn_rows, to_channel_major(pb, flip).astype(BF16)).astype(BF16)
        for s in range(per):
            block = g * per + s
            for m in range(nch):
                part = slice(s * cpad + m * rows, s * cpad + (m + 1) * rows)
                snd[m, block, 0] = pa[part]
                snd[m, n - 1 - (g * per + per - 1 - s), 1] = pb[part]

    def data_copy(m, dest, slot):
        return pltpu.make_async_remote_copy(
            src_ref=snd.at[m, dest], dst_ref=rcv.at[m, slot],
            send_sem=s_sem.at[m], recv_sem=r_sem.at[m],
            device_id={"ctx": dest},
        )

    def back_copy(m, dest, slot):
        return pltpu.make_async_remote_copy(
            src_ref=osnd.at[m, dest], dst_ref=orcv.at[m, slot],
            send_sem=os_sem.at[m], recv_sem=or_sem.at[m],
            device_id={"ctx": dest},
        )

    def all_of(m, src, dst, send_sem, recv_sem):
        return pltpu.make_async_remote_copy(
            src_ref=src.at[m, pl.ds(0, n - 1)], dst_ref=dst.at[m, pl.ds(0, n - 1)],
            send_sem=send_sem.at[m], recv_sem=recv_sem.at[m],
            device_id={"ctx": lax.rem(me + 1, n)},
        )

    def all_data(m):
        return all_of(m, snd, rcv, s_sem, r_sem)

    def all_back(m):
        return all_of(m, osnd, orcv, os_sem, or_sem)

    def each_peer(act):
        def step(o, carry):
            act(lax.rem(me + o, n))
            return carry

        lax.fori_loop(1, n, step, 0, unroll=3)

    for m in range(nch):
        each_peer(lambda peer: data_copy(m, peer, me).start())

    halo_wait((0,))
    for g in range(groups):
        ls = slice(g * LANES, (g + 1) * LANES)
        qmix[0, :, ls] = short_sum(xs, taps, 0, 0, ls)
        qmix[1, :, ls] = short_sum(xs, taps, 1, 0, ls)

    def conv(m, which, at):
        rs = pl.ds(at, 8)
        hs = pl.ds(m * rows + at, 8)
        re, im = slice(0, LANES), slice(LANES, 2 * LANES)
        if n <= 16:
            x = [(xh[which, t, rs, re], xh[which, t, rs, im]) for t in range(n)]
            tile = 4
            for t0 in range(0, n, tile):
                acc = [None] * tile
                for d in range(t0 + tile):
                    hr, hi = hh[d, hs, re], hh[d, hs, im]
                    for u in range(tile):
                        if t0 + u < d:
                            continue
                        xr, xi = x[t0 + u - d]
                        yr, yi = xr * hr - xi * hi, xr * hi + xi * hr
                        acc[u] = (yr, yi) if acc[u] is None else (acc[u][0] + yr, acc[u][1] + yi)
                for u in range(tile):
                    yh[which, t0 + u, rs, re], yh[which, t0 + u, rs, im] = acc[u]
            return

        def output(t, carry):
            def term(d, total):
                xr, xi = xh[which, t - d, rs, re], xh[which, t - d, rs, im]
                hr, hi = hh[d, hs, re], hh[d, hs, im]
                return total[0] + xr * hr - xi * hi, total[1] + xr * hi + xi * hr

            zero = jnp.zeros((8, LANES), F32)
            yh[which, t, rs, re], yh[which, t, rs, im] = lax.fori_loop(0, t + 1, term, (zero, zero))
            return carry

        lax.fori_loop(0, n, output, 0)

    steps = rows // 8
    for m in range(nch):
        all_data(m).wait_recv()
        rcv[m, me] = snd[m, me]
        for which in range(2):
            order = range(n) if which == 0 else range(n - 1, -1, -1)
            x = jnp.concatenate([rcv[m, t, which] for t in order], axis=0)
            spec = mm(x, fwd[0, 0:LANES, :]) + mm(x, fwd[1, 0:LANES, :])
            xh[which] = spec.reshape(n, rows, 2 * LANES)

        def step(i, carry):
            conv(m, i // steps, pl.multiple_of(i % steps * 8, 8))
            return carry

        lax.fori_loop(0, 2 * steps, step, 0)
        for which in range(2):
            y = yh[which].reshape(n * rows, 2 * LANES)
            high = y.astype(BF16)
            rest = (y - high.astype(F32)).astype(BF16)
            y = (mm(high, inv[0]) + mm(high, inv[1]) + mm(rest, inv[0])).astype(BF16)
            for t in range(n):
                osnd[m, t if which == 0 else n - 1 - t, which] = y[t * rows : (t + 1) * rows]
        each_peer(lambda peer: back_copy(m, peer, me).start())
        orcv[m, me] = osnd[m, me]

    for m in range(nch):
        all_back(m).wait_recv()

    for g in range(groups):
        ls = slice(g * LANES, (g + 1) * LANES)
        blocks = [g * per + s for s in range(per)]
        ma = jnp.concatenate([orcv[m, b, 0] for b in blocks for m in range(nch)], axis=0)
        mb = jnp.concatenate(
            [orcv[m, n - 1 - b, 1] for b in reversed(blocks) for m in range(nch)], axis=0
        )
        mb = mm(turn_rows, mb).astype(BF16)
        mixed = qmix[0, :, ls] * to_time_major(eye, ma) + qmix[1, :, ls] * to_time_major(flip, mb)
        mixed = to_channel_major(mixed.astype(BF16), eye)
        for s, b in enumerate(blocks):
            part = mixed[s * cpad + low : s * cpad + low + cblk]
            xf[0, 8 + b * cblk : 8 + (b + 1) * cblk, :] = part
    out[...] = xf[0, 8:held, :].astype(BF16)

    for m in range(nch):
        all_data(m).wait_send()
        all_back(m).wait_send()

    @pl.when(me < n - 1)
    def _():
        for a in range(3):
            halo(a, True).wait_send()

    @pl.when(me > 0)
    def _():
        for a in range(3):
            halo(a, False).wait_send()


def on_device(queries, key_rows, value_rows, short_taps, long_filter):
    n = lax.axis_size("ctx")
    channels, tokens = queries.shape
    cblk, length = long_filter.shape
    cpad, low, rows = dims_of(cblk)
    nch = cpad // rows
    cp = n * cpad
    taps = jnp.swapaxes(short_taps, 1, 2)
    hbm = pl.BlockSpec(memory_space=pltpu.MemorySpace.HBM)
    vmem = pl.BlockSpec(memory_space=pltpu.VMEM)
    dma = pltpu.SemaphoreType.DMA
    return pl.pallas_call(
        functools.partial(kernel, n, cblk),
        out_shape=jax.ShapeDtypeStruct((channels, tokens), BF16),
        in_specs=[hbm] * 7,
        out_specs=vmem,
        scratch_shapes=[
            pltpu.VMEM((3, channels, tokens), BF16),
            pltpu.VMEM((3, TAPS, channels), F32),
            pltpu.VMEM((cblk, length), BF16),
            dma((7,)),
            pltpu.VMEM((3, 8, cp), F32),
            pltpu.VMEM((2, 3, 8, cp), F32),
            pltpu.VMEM((3, channels + 24, LANES), F32),
            pltpu.VMEM((3, LANES + 16, cp), F32),
            pltpu.VMEM((2, LANES, cp), F32),
            pltpu.VMEM((nch, n, 2, rows, LANES), BF16),
            pltpu.VMEM((nch, n, 2, rows, LANES), BF16),
            pltpu.VMEM((nch, n, 2, rows, LANES), BF16),
            pltpu.VMEM((nch, n, 2, rows, LANES), BF16),
            pltpu.VMEM((2, 2 * LANES, 2 * LANES), BF16),
            pltpu.VMEM((2, 2 * LANES, LANES), BF16),
            pltpu.VMEM((n, cpad, 2 * LANES), F32),
            pltpu.VMEM((2, n, rows, 2 * LANES), F32),
            pltpu.VMEM((2, n, rows, 2 * LANES), F32),
            dma((2, 3)),
            dma((2, 3)),
            dma((nch,)),
            dma((nch,)),
            dma((nch,)),
            dma((nch,)),
        ],
        compiler_params=pltpu.CompilerParams(
            collective_id=0, has_side_effects=True, vmem_limit_bytes=62 * 1024 * 1024
        ),
    )(queries, key_rows, value_rows, taps, long_filter, *(jnp.asarray(x) for x in dft_tables()))


def solution(mesh):
    placed = (
        P(None, ("grp", "ctx")),
        P(None, ("grp", "ctx")),
        P(None, ("grp", "ctx")),
        P(),
        P("ctx", None),
    )
    return jax.shard_map(
        on_device, mesh=mesh, in_specs=placed, out_specs=P(None, ("grp", "ctx")), check_vma=False
    )
```

```python
import functools

import jax
import jax.numpy as jnp
import numpy as np
from jax import lax
from jax.experimental import pallas as pl
from jax.experimental.pallas import tpu as pltpu
from jax.sharding import PartitionSpec as P

TAPS = 7
LANES = 128
F32 = jnp.float32
BF16 = jnp.bfloat16


def dims_of(cblk):
    cpad = -(-cblk // 16) * 16
    low = (cpad - cblk) // 2
    even = 2 * low + cblk == cpad
    rows = 32 if even and cpad % 32 == 0 else cpad
    return cpad, low, rows


def unit(flip):
    i = lax.broadcasted_iota(jnp.int32, (LANES, LANES), 0)
    j = lax.broadcasted_iota(jnp.int32, (LANES, LANES), 1)
    j = LANES - 1 - j if flip else j
    return (i == j).astype(F32).astype(BF16)


def mirror(cblk):
    cpad, low, _ = dims_of(cblk)
    if 2 * low + cblk == cpad:
        return unit(True)
    i = lax.broadcasted_iota(jnp.int32, (LANES, LANES), 0)
    j = lax.broadcasted_iota(jnp.int32, (LANES, LANES), 1)
    blocks = i // cpad + j // cpad == LANES // cpad - 1
    return (blocks & (i % cpad + j % cpad == cblk - 1 + 2 * low)).astype(F32).astype(BF16)


def dft_tables():
    t = np.arange(2 * LANES)[:, None]
    angle = np.pi * t * (np.arange(LANES)[None] + 0.5) / LANES
    fwd = np.concatenate([np.cos(angle), -np.sin(angle)], axis=1)
    inv = fwd[LANES:].T / LANES

    def pair(x):
        high = x.astype(BF16)
        return np.stack([high, (x - high.astype(np.float64)).astype(BF16)])

    return pair(fwd), pair(inv)


def mm(a, b):
    return lax.dot_general(a, b, (((1,), (0,)), ((), ())), preferred_element_type=F32)


def to_time_major(mat, x):
    return lax.dot_general(mat, x, (((1,), (1,)), ((), ())), preferred_element_type=F32)


def to_channel_major(x, mat):
    return lax.dot_general(x, mat, (((0,), (0,)), ((), ())), preferred_element_type=F32)


def short_sum(xs, taps, way, which, lanes, row, count):
    total = None
    for j in range(TAPS):
        start = 8 + row - j if way == 0 else 8 + row + j
        term = taps[way, which, j : j + 1, lanes] * xs[which, start : start + count, lanes]
        total = term if total is None else total + term
    return total


def kernel(
    n, parts, cblk, q_hbm, k_hbm, v_hbm, taps_hbm, filt_hbm, fwd_hbm, inv_hbm, out,
    xin, tin, filt, other, in_sem, alt, taps, xf, xs, qmix, prod, snd, near, far, osnd, orcv, psnd, prcv,
    fwd, inv, hown, hother, xh, yh,
    hs_sem, hr_sem, s_sem, r_sem, fs_sem, fr_sem, os_sem, or_sem, ps_sem, pr_sem, zs_sem, zr_sem, xs_sem, xr_sem,
):
    cpad, low, rows = dims_of(cblk)
    half = n // 2
    nch = 2 * cpad // rows
    cp = n * cpad
    groups = cp // LANES
    per_chunk = groups // nch
    dests = LANES // rows
    own = nch // 2
    span = other.shape[-1]
    channels = n * cblk
    held = 8 + channels
    me = lax.axis_index("ctx")
    grp = lax.axis_index("grp")
    side = me // half
    r = lax.rem(me, half)
    slot = jnp.where(side == 0, r, half - 1 - r)
    home = side * half
    away = (1 - side) * half

    barrier = pltpu.get_barrier_semaphore()

    def greet(o, carry):
        pl.semaphore_signal(barrier, inc=1, device_id={"ctx": lax.rem(me + o, n)})
        return carry

    lax.fori_loop(1, n, greet, 0)
    for o in range(1, parts):
        pl.semaphore_signal(barrier, inc=1, device_id={"grp": lax.rem(grp + o, parts)})

    loads = [
        pltpu.make_async_copy(src, dst, in_sem.at[i])
        for i, (src, dst) in enumerate((
            (q_hbm, xin.at[0]), (k_hbm, xin.at[1]), (v_hbm, xin.at[2]),
            (taps_hbm, tin), (fwd_hbm, fwd), (inv_hbm, inv), (filt_hbm, filt),
        ))
    ]
    for i in (1, 2, 3, 0, 4, 5, 6):
        loads[i].start()

    eye = unit(False)
    flip = unit(True)
    turn_rows = mirror(cblk)
    taps[...] = jnp.zeros((2, 3, 8, cp), F32)
    alt[...] = jnp.zeros((3, 8, cp), F32)
    for a in range(3):
        xf[a, 0:8, :] = jnp.zeros((8, LANES), F32)
        xf[a, held : held + 16, :] = jnp.zeros((16, LANES), F32)

    @pl.when(me == 0)
    def _():
        xs[:, 0:8, :] = jnp.zeros((3, 8, cp), F32)

    @pl.when(me == n - 1)
    def _():
        xs[:, 8 + LANES : 16 + LANES, :] = jnp.zeros((3, 8, cp), F32)

    pieces = [
        ((d + half * (at // cpad)) * cblk, at % cpad) for at in range(0, 2 * cpad, rows) for d in range(half)
    ]

    def turn(a):
        loads[a].wait()
        xf[a, 8:held, :] = xin[a].astype(F32)
        for g in range(groups):
            starts = [8 + first - low + at for first, at in pieces[g * dests : (g + 1) * dests]]
            block = jnp.concatenate([xf[a, i : i + rows, :] for i in starts], axis=0).astype(BF16)
            xs[a, 8 : 8 + LANES, g * LANES : (g + 1) * LANES] = to_time_major(eye, block)

    def halo(a, up):
        if up:
            return pltpu.make_async_remote_copy(
                src_ref=xs.at[a, pl.ds(LANES, 8)], dst_ref=xs.at[a, pl.ds(0, 8)],
                send_sem=hs_sem.at[0, a], recv_sem=hr_sem.at[0, a],
                device_id={"ctx": lax.rem(me + 1, n)},
            )
        return pltpu.make_async_remote_copy(
            src_ref=xs.at[a, pl.ds(8, 8)], dst_ref=xs.at[a, pl.ds(8 + LANES, 8)],
            send_sem=hs_sem.at[1, a], recv_sem=hr_sem.at[1, a],
            device_id={"ctx": lax.rem(me + n - 1, n)},
        )

    def halo_wait(arrays):
        @pl.when(me > 0)
        def _():
            for a in arrays:
                halo(a, True).wait_recv()

        @pl.when(me < n - 1)
        def _():
            for a in arrays:
                halo(a, False).wait_recv()

    def halo_start(arrays):
        @pl.when(me < n - 1)
        def _():
            for a in arrays:
                halo(a, True).start()

        @pl.when(me > 0)
        def _():
            for a in arrays:
                halo(a, False).start()

    def filter_over():
        return pltpu.make_async_remote_copy(
            src_ref=filt_hbm.at[:, pl.ds(pl.multiple_of(grp * span, LANES), span)], dst_ref=other.at[grp],
            send_sem=zs_sem, recv_sem=zr_sem, device_id={"ctx": away + r},
        )

    def filter_across(o, share):
        return pltpu.make_async_remote_copy(
            src_ref=other.at[share], dst_ref=other.at[share], send_sem=xs_sem.at[o], recv_sem=xr_sem.at[o],
            device_id={"grp": lax.rem(grp + o, parts)},
        )

    pl.semaphore_wait(barrier, n - 1 + parts - 1)
    filter_over().start()
    turn(1)
    turn(2)
    halo_start((1, 2))
    turn(0)
    halo_start((0,))
    loads[3].wait()
    for ref, shift in ((taps.at[0], low), (alt, cpad - cblk - low)):
        for b, (first, row) in enumerate(pieces):
            base = first - shift + row
            lo, hi = max(base, 0), min(base + rows, channels)
            at = b * rows + lo - base
            ref[:, 0:TAPS, at : at + hi - lo] = tin[:, :, lo:hi]
    turner = unit(True).astype(F32)
    for g in range(groups):
        source = alt[:, :, cp - (g + 1) * LANES : cp - g * LANES].reshape(24, LANES)
        taps[1, :, :, g * LANES : (g + 1) * LANES] = jnp.dot(
            source, turner, precision=lax.Precision.HIGHEST, preferred_element_type=F32
        ).reshape(3, 8, LANES)

    def product(g, row, count, way):
        ls = slice(g * LANES, (g + 1) * LANES)
        prod[way, row : row + count, ls] = short_sum(xs, taps, way, 1, ls, row, count) * short_sum(
            xs, taps, way, 2, ls, row, count
        )

    for g in [*range(groups // 2, groups), *range(groups // 2)]:
        product(g, 8, LANES - 8, 0)
        product(g, 0, LANES - 8, 1)

    def rel(m):
        return lax.rem(m + side * own, nch)

    first, second = side, 1 - side

    def turned(i, flag):
        return jnp.where(side == flag, i, own - 1 - i)

    def near_copy(m, j):
        return pltpu.make_async_remote_copy(
            src_ref=snd.at[m, j], dst_ref=near.at[m, slot],
            send_sem=s_sem.at[m], recv_sem=r_sem.at[m], device_id={"ctx": home + j},
        )

    def far_copy(i, j):
        return pltpu.make_async_remote_copy(
            src_ref=snd.at[own + i, j, 0], dst_ref=far.at[i, slot],
            send_sem=fs_sem.at[i], recv_sem=fr_sem.at[i], device_id={"ctx": away + j},
        )

    def place_of(j):
        return jnp.where(side == 0, j, half - 1 - j)

    def back_copy(m, j):
        return pltpu.make_async_remote_copy(
            src_ref=osnd.at[m, place_of(j)], dst_ref=orcv.at[m, r],
            send_sem=os_sem.at[m], recv_sem=or_sem.at[m], device_id={"ctx": home + j},
        )

    def part_copy(i, j):
        return pltpu.make_async_remote_copy(
            src_ref=psnd.at[i, place_of(j)], dst_ref=prcv.at[i, r],
            send_sem=ps_sem.at[i], recv_sem=pr_sem.at[i], device_id={"ctx": away + j},
        )

    def all_of(src, dst, send_sem, recv_sem):
        return pltpu.make_async_remote_copy(
            src_ref=src, dst_ref=dst, send_sem=send_sem, recv_sem=recv_sem,
            device_id={"ctx": lax.rem(me + 1, n)},
        )

    def all_near(m):
        some = pl.ds(0, half - 1)
        return all_of(snd.at[m, some], near.at[m, some], s_sem.at[m], r_sem.at[m])

    def all_far(i):
        return all_of(far.at[i], far.at[i], fs_sem.at[i], fr_sem.at[i])

    def all_part(i):
        return all_of(psnd.at[i], prcv.at[i], ps_sem.at[i], pr_sem.at[i])

    def all_back(m):
        some = pl.ds(0, half - 1)
        return all_of(osnd.at[m, some], orcv.at[m, some], os_sem.at[m], or_sem.at[m])

    def each(first, act):
        def step(o, carry):
            act(lax.rem(r + o, half))
            return carry

        lax.fori_loop(first, half, step, 0, unroll=True if half <= 8 else 1)

    halo_wait((1, 2))
    for m in [*range(own, nch), *range(own)]:
        for g in range(m * per_chunk, (m + 1) * per_chunk):
            ls = slice(g * LANES, (g + 1) * LANES)
            product(g, 0, 8, 0)
            product(g, LANES - 8, 8, 1)
            pa = to_channel_major(prod[0, :, ls].astype(BF16), eye).astype(BF16)
            pb = to_channel_major(prod[1, :, ls].astype(BF16), flip).astype(BF16)
            pb = mm(turn_rows, pb).astype(BF16)
            at = (g - m * per_chunk) * dests
            for s in range(dests):
                piece = slice(s * rows, (s + 1) * rows)
                snd[rel(m), at + s, first] = pa[piece]
                snd[rel(nch - 1 - m), half - at - dests + s, second] = pb[piece]
        if m == nch - 1:
            for i in range(own):
                each(0, lambda j: far_copy(turned(i, 0), j).start())
    for i in range(own):
        each(1, lambda j: near_copy(turned(i, 1), j).start())
    for i in range(own):
        each(1, lambda j: near_copy(own + turned(i, 0), j).start())

    halo_wait((0,))
    for g in range(groups):
        ls = slice(g * LANES, (g + 1) * LANES)
        qmix[0, :, ls] = short_sum(xs, taps, 0, 0, ls, 0, LANES)
        qmix[1, :, ls] = short_sum(xs, taps, 1, 0, ls, 0, LANES)

    for i in (4, 5, 6):
        loads[i].wait()
    place = lax.broadcasted_iota(jnp.int32, (cpad, cblk), 0) - lax.broadcasted_iota(jnp.int32, (cpad, cblk), 1)
    place = (place == low).astype(F32).astype(BF16)

    def spectra(dst, shares):
        lag = [jnp.zeros((cpad, LANES), BF16)]
        for share in shares:
            padded = mm(place, share).astype(BF16)
            lag += [padded[:, at : at + LANES] for at in range(0, share.shape[-1], LANES)]
        for d in range(len(lag) - 1):
            line = jnp.concatenate([lag[d], lag[d + 1]], axis=1)
            dst[d] = mm(line, fwd[0]) + mm(line, fwd[1])

    spectra(hown, [filt[...]])
    filter_over().wait_recv()
    for o in range(1, parts):
        filter_across(o, grp).start()

    re, im = slice(0, LANES), slice(LANES, 2 * LANES)

    def pair(ref, *index):
        return ref[(*index, re)], ref[(*index, im)]

    def times(x, h):
        return x[0] * h[0] - x[1] * h[1], x[0] * h[1] + x[1] * h[0]

    def block_sums(spec, top, out_at, x_at, at, back=None, more=None):
        rs = pl.ds(at, 8)
        hs = pl.ds(top + at, 8)
        ahead, behind = (x_at, back) if more is None else (None, x_at)
        if half > 8:
            def output(t, carry):
                def term(seq, shift, d, total):
                    y = times(pair(xh, *seq, t + shift - d, rs), pair(spec, d, hs))
                    return total[0] + y[0], total[1] + y[1]

                total = (jnp.zeros((8, LANES), F32),) * 2
                if ahead is not None:
                    total = lax.fori_loop(0, t + 1, functools.partial(term, ahead, 0), total)
                if behind is not None:
                    total = lax.fori_loop(t + 1, t + half + 1, functools.partial(term, behind, half), total)
                yh[out_at, t, rs, re], yh[out_at, t, rs, im] = total
                return carry

            lax.fori_loop(0, half, output, 0)
            return
        x = {}
        if behind is not None:
            x.update({t: pair(xh, *behind, t, rs) for t in range(half)})
        if ahead is not None:
            x.update({half + t: pair(xh, *ahead, t, rs) for t in range(half)})
        tile = 4
        for t0 in range(half, 2 * half, tile):
            acc = [None] * tile
            for d in range(2 * half):
                used = [u for u in range(tile) if t0 + u - d in x]
                if not used:
                    continue
                h = pair(spec, d, hs)
                for u in used:
                    y = times(x[t0 + u - d], h)
                    acc[u] = y if acc[u] is None else (acc[u][0] + y[0], acc[u][1] + y[1])
            for u in range(tile):
                t = t0 - half + u
                yh[out_at, t, rs, re], yh[out_at, t, rs, im] = acc[u]

    def transform(dst, blocks):
        x = jnp.concatenate(blocks, axis=0)
        spec = mm(x, fwd[0, 0:LANES, :]) + mm(x, fwd[1, 0:LANES, :])
        xh[dst] = spec.reshape(half, rows, 2 * LANES)

    def result(which):
        y = yh[which].reshape(half * rows, 2 * LANES)
        high = y.astype(BF16)
        rest = (y - high.astype(F32)).astype(BF16)
        y = (mm(high, inv[0]) + mm(high, inv[1]) + mm(rest, inv[0])).astype(BF16)
        return [y[t * rows : (t + 1) * rows] for t in range(half)]

    def octets(body):
        def step(i, carry):
            body(pl.multiple_of(i * 8, 8))
            return carry

        lax.fori_loop(0, rows // 8, step, 0)

    def receive(m):
        all_near(m).wait_recv()
        near[m, slot] = snd[m, r]

    def send_back(m):
        for t, y in enumerate(result(0)):
            osnd[m, t, 0] = y
        for t, y in enumerate(result(1)):
            osnd[m, half - 1 - t, 1] = y
        each(1, lambda j: back_copy(m, j).start())
        orcv[m, r] = osnd[m, slot]

    eye2 = jnp.concatenate([eye.astype(F32), jnp.where(side == 1, eye.astype(F32), 0.0)], axis=1).astype(BF16)
    flip2 = jnp.concatenate([flip.astype(F32), jnp.where(side == 0, flip.astype(F32), 0.0)], axis=1).astype(BF16)

    def mix(m):
        for g in range(m * per_chunk, (m + 1) * per_chunk):
            ls = slice(g * LANES, (g + 1) * LANES)
            at = (g - m * per_chunk) * dests
            ma = jnp.concatenate([orcv[rel(m), at + s, first] for s in range(dests)], axis=0)
            mb = jnp.concatenate(
                [orcv[rel(nch - 1 - m), half - at - dests + s, second] for s in range(dests)], axis=0
            )
            mb = mm(turn_rows, mb).astype(BF16)
            if m < own:
                rest = jnp.concatenate(
                    [prcv[turned(m, 1), jnp.where(side == 1, at, half - at - dests) + s] for s in range(dests)], axis=0
                )
                ma = to_time_major(eye2, jnp.concatenate([ma, rest], axis=1))
                rest = mm(turn_rows, rest).astype(BF16)
                mb = to_time_major(flip2, jnp.concatenate([mb, rest], axis=1))
            else:
                ma, mb = to_time_major(eye, ma), to_time_major(flip, mb)
            mixed = qmix[0, :, ls] * ma + qmix[1, :, ls] * mb
            mixed = to_channel_major(mixed.astype(BF16), eye)
            for s, (start, row) in enumerate(pieces[g * dests : (g + 1) * dests]):
                lo, hi = max(row, low), min(row + rows, low + cblk)
                to = 8 + start - low
                xf[0, to + lo : to + hi, :] = mixed[s * rows + lo - row : s * rows + hi - row]

    for i in range(own):
        m = turned(i, 1)
        receive(m)
        transform((i, 0), [near[m, t, 0] for t in range(half)])
        octets(lambda at: block_sums(hown, m * rows, 0, (i, 0), at, more=True))
        for t, y in enumerate(result(0)):
            psnd[m, t] = y
        each(0, lambda j: part_copy(m, j).start())
    for i in range(own):
        m = turned(i, 1)
        transform((i, 1), [near[m, half - 1 - t, 1] for t in range(half)])
        all_far(m).wait_recv()
        transform((i, 2), [far[m, t] for t in range(half)])

        def both(at):
            block_sums(hown, m * rows, 0, (i, 0), at)
            block_sums(hown, m * rows, 1, (i, 1), at, back=(i, 2))

        octets(both)
        send_back(m)
    for o in range(1, parts):
        filter_across(o, lax.rem(grp + parts - o, parts)).wait_recv()
    spectra(hother, [other[g] for g in range(parts)])
    for i in range(own):
        m = turned(i, 0)
        receive(own + m)
        transform((0, 0), [near[own + m, t, 0] for t in range(half)])
        transform((0, 1), [near[own + m, half - 1 - t, 1] for t in range(half)])

        def both(at):
            block_sums(hother, m * rows, 0, (0, 0), at)
            block_sums(hother, m * rows, 1, (0, 1), at)

        octets(both)
        send_back(own + m)
    for i in range(own):
        all_back(turned(i, 1)).wait_recv()
    for i in range(own):
        all_back(own + turned(i, 0)).wait_recv()
        mix(own + i)
        all_part(turned(i, 0)).wait_recv()
        mix(own - 1 - i)
    out[...] = xf[0, 8:held, :].astype(BF16)

    for m in range(nch):
        all_near(m).wait_send()
        all_back(m).wait_send()
    for i in range(own):
        all_far(i).wait_send()
        all_part(i).wait_send()
    filter_over().wait_send()
    for o in range(1, parts):
        filter_across(o, grp).wait_send()

    @pl.when(me < n - 1)
    def _():
        for a in range(3):
            halo(a, True).wait_send()

    @pl.when(me > 0)
    def _():
        for a in range(3):
            halo(a, False).wait_send()


def on_device(queries, key_rows, value_rows, short_taps, long_filter):
    n = lax.axis_size("ctx")
    parts = lax.axis_size("grp")
    channels, tokens = queries.shape
    cblk, length = long_filter.shape
    cpad, low, rows = dims_of(cblk)
    half = n // 2
    nch = 2 * cpad // rows
    own = nch // 2
    cp = n * cpad
    taps = jnp.swapaxes(short_taps, 1, 2)
    hbm = pl.BlockSpec(memory_space=pltpu.MemorySpace.HBM)
    vmem = pl.BlockSpec(memory_space=pltpu.VMEM)
    dma = pltpu.SemaphoreType.DMA
    return pl.pallas_call(
        functools.partial(kernel, n, parts, cblk),
        out_shape=jax.ShapeDtypeStruct((channels, tokens), BF16),
        in_specs=[hbm] * 7,
        out_specs=vmem,
        scratch_shapes=[
            pltpu.VMEM((3, channels, tokens), BF16),
            pltpu.VMEM((3, TAPS, channels), F32),
            pltpu.VMEM((cblk, length), BF16),
            pltpu.VMEM((parts, cblk, half * LANES // parts), BF16),
            dma((7,)),
            pltpu.VMEM((3, 8, cp), F32),
            pltpu.VMEM((2, 3, 8, cp), F32),
            pltpu.VMEM((3, channels + 24, LANES), F32),
            pltpu.VMEM((3, LANES + 16, cp), F32),
            pltpu.VMEM((2, LANES, cp), F32),
            pltpu.VMEM((2, LANES, cp), F32),
            pltpu.VMEM((nch, half, 2, rows, LANES), BF16),
            pltpu.VMEM((nch, half, 2, rows, LANES), BF16),
            pltpu.VMEM((own, half, rows, LANES), BF16),
            pltpu.VMEM((nch, half, 2, rows, LANES), BF16),
            pltpu.VMEM((nch, half, 2, rows, LANES), BF16),
            pltpu.VMEM((own, half, rows, LANES), BF16),
            pltpu.VMEM((own, half, rows, LANES), BF16),
            pltpu.VMEM((2, 2 * LANES, 2 * LANES), BF16),
            pltpu.VMEM((2, 2 * LANES, LANES), BF16),
            pltpu.VMEM((n, cpad, 2 * LANES), F32),
            pltpu.VMEM((half, cpad, 2 * LANES), F32),
            pltpu.VMEM((own, 3, half, rows, 2 * LANES), F32),
            pltpu.VMEM((2, half, rows, 2 * LANES), F32),
            dma((2, 3)),
            dma((2, 3)),
            dma((nch,)),
            dma((nch,)),
            dma((own,)),
            dma((own,)),
            dma((nch,)),
            dma((nch,)),
            dma((own,)),
            dma((own,)),
            dma(()),
            dma(()),
            dma((parts,)),
            dma((parts,)),
        ],
        compiler_params=pltpu.CompilerParams(
            collective_id=0, has_side_effects=True, vmem_limit_bytes=62 * 1024 * 1024
        ),
    )(queries, key_rows, value_rows, taps, long_filter, *(jnp.asarray(x) for x in dft_tables()))


def solution(mesh):
    placed = (
        P(None, ("grp", "ctx")),
        P(None, ("grp", "ctx")),
        P(None, ("grp", "ctx")),
        P(),
        P("ctx", None),
    )
    return jax.shard_map(
        on_device, mesh=mesh, in_specs=placed, out_specs=P(None, ("grp", "ctx")), check_vma=False
    )
```

```python
import functools

import jax
import jax.numpy as jnp
import numpy as np
from jax import lax
from jax.experimental import pallas as pl
from jax.experimental.pallas import tpu as pltpu
from jax.sharding import PartitionSpec as P

TAPS = 7
LANES = 128
F32 = jnp.float32
BF16 = jnp.bfloat16


def dims_of(cblk):
    cpad = -(-cblk // 16) * 16
    low = (cpad - cblk) // 2
    even = 2 * low + cblk == cpad
    rows = 32 if even and cpad % 32 == 0 else cpad
    return cpad, low, rows


def unit(flip):
    i = lax.broadcasted_iota(jnp.int32, (LANES, LANES), 0)
    j = lax.broadcasted_iota(jnp.int32, (LANES, LANES), 1)
    j = LANES - 1 - j if flip else j
    return (i == j).astype(F32).astype(BF16)


def dft_tables():
    t = np.arange(2 * LANES)[:, None]
    angle = np.pi * t * (np.arange(LANES)[None] + 0.5) / LANES
    fwd = np.concatenate([np.cos(angle), -np.sin(angle)], axis=1)
    inv = fwd[LANES:].T / LANES

    def pair(x):
        high = x.astype(BF16)
        return np.stack([high, (x - high.astype(np.float64)).astype(BF16)])

    return pair(fwd), np.stack([pair(inv), pair(inv[:, ::-1])])


def mm(a, b):
    return lax.dot_general(a, b, (((1,), (0,)), ((), ())), preferred_element_type=F32)


def to_time_major(mat, x):
    return lax.dot_general(mat, x, (((1,), (1,)), ((), ())), preferred_element_type=F32)


def to_channel_major(x, mat):
    return lax.dot_general(x, mat, (((0,), (0,)), ((), ())), preferred_element_type=F32)


def short_sum(xs, taps, way, which, lanes, row, count):
    total = None
    for j in range(TAPS):
        start = 8 + row - j if way == 0 else 8 + row + j
        term = taps[way, which, j : j + 1, lanes] * xs[which, start : start + count, lanes]
        total = term if total is None else total + term
    return total


def kernel(
    n, parts, cblk, q_hbm, k_hbm, v_hbm, taps_hbm, filt_hbm, fwd_hbm, inv_hbm, out,
    xin, tin, filt, other, in_sem, alt, taps, xf, xs, qmix, prod, snd, near, far, osnd, orcv, psnd, prcv,
    fwd, inv, hown, hother, xh, yh,
    hs_sem, hr_sem, s_sem, r_sem, fs_sem, fr_sem, os_sem, or_sem, ps_sem, pr_sem, zs_sem, zr_sem, xs_sem, xr_sem,
):
    cpad, low, rows = dims_of(cblk)
    half = n // 2
    nch = 2 * cpad // rows
    cp = n * cpad
    groups = cp // LANES
    per_chunk = groups // nch
    dests = LANES // rows
    own = nch // 2
    span = other.shape[-1]
    channels = n * cblk
    held = 8 + channels
    me = lax.axis_index("ctx")
    grp = lax.axis_index("grp")
    side = me // half
    r = lax.rem(me, half)
    slot = jnp.where(side == 0, r, half - 1 - r)
    home = side * half
    away = (1 - side) * half

    loads = [
        pltpu.make_async_copy(src, dst, in_sem.at[i])
        for i, (src, dst) in enumerate((
            (q_hbm, xin.at[0]), (k_hbm, xin.at[1]), (v_hbm, xin.at[2]),
            (taps_hbm, tin), (fwd_hbm, fwd), (inv_hbm, inv), (filt_hbm, filt),
        ))
    ]
    for i in (1, 2, 3, 0, 4, 5, 6):
        loads[i].start()

    barrier = pltpu.get_barrier_semaphore()

    def greet(o, carry):
        pl.semaphore_signal(barrier, inc=1, device_id={"ctx": lax.rem(me + o, n)})
        return carry

    lax.fori_loop(1, n, greet, 0)
    for o in range(1, parts):
        pl.semaphore_signal(barrier, inc=1, device_id={"grp": lax.rem(grp + o, parts)})

    eye = unit(False)
    flip = unit(True)
    taps[...] = jnp.zeros((2, 3, 8, cp), F32)
    alt[...] = jnp.zeros((3, 8, cp), F32)
    for a in range(3):
        xf[a, 0:8, :] = jnp.zeros((8, LANES), F32)
        xf[a, held : held + 16, :] = jnp.zeros((16, LANES), F32)

    @pl.when(me == 0)
    def _():
        xs[:, 0:8, :] = jnp.zeros((3, 8, cp), F32)

    @pl.when(me == n - 1)
    def _():
        xs[:, 8 + LANES : 16 + LANES, :] = jnp.zeros((3, 8, cp), F32)

    pieces = [
        ((d + half * (at // cpad)) * cblk, at % cpad) for at in range(0, 2 * cpad, rows) for d in range(half)
    ]

    def turn(a):
        loads[a].wait()
        xf[a, 8:held, :] = xin[a].astype(F32)
        for g in range(groups):
            starts = [8 + first - low + at for first, at in pieces[g * dests : (g + 1) * dests]]
            block = jnp.concatenate([xf[a, i : i + rows, :] for i in starts], axis=0).astype(BF16)
            xs[a, 8 : 8 + LANES, g * LANES : (g + 1) * LANES] = to_time_major(eye, block)

    def halo(a, up):
        if up:
            return pltpu.make_async_remote_copy(
                src_ref=xs.at[a, pl.ds(LANES, 8)], dst_ref=xs.at[a, pl.ds(0, 8)],
                send_sem=hs_sem.at[0, a], recv_sem=hr_sem.at[0, a],
                device_id={"ctx": lax.rem(me + 1, n)},
            )
        return pltpu.make_async_remote_copy(
            src_ref=xs.at[a, pl.ds(8, 8)], dst_ref=xs.at[a, pl.ds(8 + LANES, 8)],
            send_sem=hs_sem.at[1, a], recv_sem=hr_sem.at[1, a],
            device_id={"ctx": lax.rem(me + n - 1, n)},
        )

    def halo_wait(arrays):
        @pl.when(me > 0)
        def _():
            for a in arrays:
                halo(a, True).wait_recv()

        @pl.when(me < n - 1)
        def _():
            for a in arrays:
                halo(a, False).wait_recv()

    def halo_start(arrays):
        @pl.when(me < n - 1)
        def _():
            for a in arrays:
                halo(a, True).start()

        @pl.when(me > 0)
        def _():
            for a in arrays:
                halo(a, False).start()

    def filter_over():
        return pltpu.make_async_remote_copy(
            src_ref=filt_hbm.at[:, pl.ds(pl.multiple_of(grp * span, LANES), span)], dst_ref=other.at[grp],
            send_sem=zs_sem, recv_sem=zr_sem, device_id={"ctx": away + r},
        )

    def filter_across(o, share):
        return pltpu.make_async_remote_copy(
            src_ref=other.at[share], dst_ref=other.at[share], send_sem=xs_sem.at[o], recv_sem=xr_sem.at[o],
            device_id={"grp": lax.rem(grp + o, parts)},
        )

    pl.semaphore_wait(barrier, n - 1 + parts - 1)
    filter_over().start()
    turn(1)
    turn(2)
    halo_start((1, 2))
    turn(0)
    halo_start((0,))
    loads[3].wait()
    for ref, shift in ((taps.at[0], low), (alt, cpad - cblk - low)):
        for b, (first, row) in enumerate(pieces):
            base = first - shift + row
            lo, hi = max(base, 0), min(base + rows, channels)
            at = b * rows + lo - base
            ref[:, 0:TAPS, at : at + hi - lo] = tin[:, :, lo:hi]
    turner = unit(True).astype(F32)
    for g in range(groups):
        source = alt[:, :, cp - (g + 1) * LANES : cp - g * LANES].reshape(24, LANES)
        taps[1, :, :, g * LANES : (g + 1) * LANES] = jnp.dot(
            source, turner, precision=lax.Precision.HIGHEST, preferred_element_type=F32
        ).reshape(3, 8, LANES)

    def product(g, row, count, way):
        ls = slice(g * LANES, (g + 1) * LANES)
        prod[way, row : row + count, ls] = short_sum(xs, taps, way, 1, ls, row, count) * short_sum(
            xs, taps, way, 2, ls, row, count
        )

    for g in [*range(groups // 2, groups), *range(groups // 2)]:
        product(g, 8, LANES - 8, 0)
        product(g, 0, LANES - 8, 1)

    def rel(m):
        return lax.rem(m + side * own, nch)

    first, second = side, 1 - side

    def near_copy(m, j):
        return pltpu.make_async_remote_copy(
            src_ref=snd.at[m, j], dst_ref=near.at[m, slot],
            send_sem=s_sem.at[m], recv_sem=r_sem.at[m], device_id={"ctx": home + j},
        )

    def far_copy(i, j):
        return pltpu.make_async_remote_copy(
            src_ref=snd.at[own + i, j, 0], dst_ref=far.at[i, slot],
            send_sem=fs_sem.at[i], recv_sem=fr_sem.at[i], device_id={"ctx": away + j},
        )

    def place_of(j):
        return jnp.where(side == 0, j, half - 1 - j)

    def back_copy(m, j):
        return pltpu.make_async_remote_copy(
            src_ref=osnd.at[m, place_of(j)], dst_ref=orcv.at[m, r],
            send_sem=os_sem.at[m], recv_sem=or_sem.at[m], device_id={"ctx": home + j},
        )

    def part_copy(i, j):
        return pltpu.make_async_remote_copy(
            src_ref=psnd.at[i, place_of(j)], dst_ref=prcv.at[i, r],
            send_sem=ps_sem.at[i], recv_sem=pr_sem.at[i], device_id={"ctx": away + j},
        )

    def all_of(src, dst, send_sem, recv_sem):
        return pltpu.make_async_remote_copy(
            src_ref=src, dst_ref=dst, send_sem=send_sem, recv_sem=recv_sem,
            device_id={"ctx": lax.rem(me + 1, n)},
        )

    def all_near(m):
        some = pl.ds(0, half - 1)
        return all_of(snd.at[m, some], near.at[m, some], s_sem.at[m], r_sem.at[m])

    def all_far(i):
        return all_of(far.at[i], far.at[i], fs_sem.at[i], fr_sem.at[i])

    def all_part(i):
        return all_of(psnd.at[i], prcv.at[i], ps_sem.at[i], pr_sem.at[i])

    def all_back(m):
        some = pl.ds(0, half - 1)
        return all_of(osnd.at[m, some], orcv.at[m, some], os_sem.at[m], or_sem.at[m])

    def each(first, act):
        def step(o, carry):
            act(lax.rem(r + o, half))
            return carry

        lax.fori_loop(first, half, step, 0, unroll=True if half <= 8 else 1)

    halo_wait((1, 2))
    for m in [*range(own, nch), *range(own)]:
        for g in range(m * per_chunk, (m + 1) * per_chunk):
            ls = slice(g * LANES, (g + 1) * LANES)
            product(g, 0, 8, 0)
            product(g, LANES - 8, 8, 1)
            pa = to_channel_major(prod[0, :, ls].astype(BF16), eye).astype(BF16)
            pb = to_channel_major(prod[1, :, ls].astype(BF16), flip).astype(BF16)
            at = (g - m * per_chunk) * dests
            for s in range(dests):
                piece = slice(s * rows, (s + 1) * rows)
                snd[rel(m), at + s, first] = pa[piece]
                snd[rel(m + own), half - 1 - at - s, second] = pb[piece]
    for i in range(own):
        each(1, lambda j: near_copy(i, j).start())
    for i in range(own):
        each(0, lambda j: far_copy(i, j).start())
    for i in range(own):
        each(1, lambda j: near_copy(own + i, j).start())

    halo_wait((0,))
    for g in range(groups):
        ls = slice(g * LANES, (g + 1) * LANES)
        for way in range(2):
            q = short_sum(xs, taps, way, 0, ls, 0, LANES)
            high = q.astype(BF16)
            rest = (q - high.astype(F32)).astype(BF16)
            qmix[way, ls, :] = to_channel_major(high, eye) + to_channel_major(rest, eye)

    for i in (4, 5, 6):
        loads[i].wait()
    row = lax.broadcasted_iota(jnp.int32, (cpad, cblk), 0)
    col = lax.broadcasted_iota(jnp.int32, (cpad, cblk), 1)
    places = [
        (row == jnp.where(side == of, low + col, low + cblk - 1 - col)).astype(F32).astype(BF16) for of in range(2)
    ]

    def spectra(dst, shares):
        for which, place in enumerate(places):
            lag = [jnp.zeros((cpad, LANES), BF16)]
            for share in shares:
                padded = mm(place, share).astype(BF16)
                lag += [padded[:, at : at + LANES] for at in range(0, share.shape[-1], LANES)]
            for d in range(len(lag) - 1):
                line = jnp.concatenate([lag[d], lag[d + 1]], axis=1)
                dst[which, d] = mm(line, fwd[0]) + mm(line, fwd[1])

    spectra(hown, [filt[...]])
    filter_over().wait_recv()
    for o in range(1, parts):
        filter_across(o, grp).start()

    re, im = slice(0, LANES), slice(LANES, 2 * LANES)

    def pair(ref, *index):
        return ref[(*index, re)], ref[(*index, im)]

    def times(x, h):
        return x[0] * h[0] - x[1] * h[1], x[0] * h[1] + x[1] * h[0]

    def block_sums(spec, kind, top, out_at, x_at, at, back=None, more=None):
        rs = pl.ds(at, 8)
        hs = pl.ds(top + at, 8)
        ahead, behind = (x_at, back) if more is None else (None, x_at)
        if half > 8:
            def output(t, carry):
                def term(seq, shift, d, total):
                    y = times(pair(xh, *seq, t + shift - d, rs), pair(spec, kind, d, hs))
                    return total[0] + y[0], total[1] + y[1]

                total = (jnp.zeros((8, LANES), F32),) * 2
                if ahead is not None:
                    total = lax.fori_loop(0, t + 1, functools.partial(term, ahead, 0), total)
                if behind is not None:
                    total = lax.fori_loop(t + 1, t + half + 1, functools.partial(term, behind, half), total)
                yh[out_at, t, rs, re], yh[out_at, t, rs, im] = total
                return carry

            lax.fori_loop(0, half, output, 0)
            return
        x = {}
        if behind is not None:
            x.update({t: pair(xh, *behind, t, rs) for t in range(half)})
        if ahead is not None:
            x.update({half + t: pair(xh, *ahead, t, rs) for t in range(half)})
        tile = 4
        for t0 in range(half, 2 * half, tile):
            acc = [None] * tile
            for d in range(2 * half):
                used = [u for u in range(tile) if t0 + u - d in x]
                if not used:
                    continue
                h = pair(spec, kind, d, hs)
                for u in used:
                    y = times(x[t0 + u - d], h)
                    acc[u] = y if acc[u] is None else (acc[u][0] + y[0], acc[u][1] + y[1])
            for u in range(tile):
                t = t0 - half + u
                yh[out_at, t, rs, re], yh[out_at, t, rs, im] = acc[u]

    def transform(dst, blocks):
        x = jnp.concatenate(blocks, axis=0)
        spec = mm(x, fwd[0, 0:LANES, :]) + mm(x, fwd[1, 0:LANES, :])
        xh[dst] = spec.reshape(half, rows, 2 * LANES)

    def result(which):
        y = yh[which].reshape(half * rows, 2 * LANES)
        high = y.astype(BF16)
        rest = (y - high.astype(F32)).astype(BF16)
        way = first if which == 0 else second
        y = (mm(high, inv[way, 0]) + mm(high, inv[way, 1]) + mm(rest, inv[way, 0])).astype(BF16)
        return [y[t * rows : (t + 1) * rows] for t in range(half)]

    def octets(body):
        def step(i, carry):
            body(pl.multiple_of(i * 8, 8))
            return carry

        lax.fori_loop(0, rows // 8, step, 0)

    def receive(m):
        all_near(m).wait_recv()
        near[m, slot] = snd[m, r]

    def send_back(m):
        for t, y in enumerate(result(0)):
            osnd[m, t, 0] = y
        for t, y in enumerate(result(1)):
            osnd[m, half - 1 - t, 1] = y
        each(1, lambda j: back_copy(m, j).start())
        orcv[m, r] = osnd[m, slot]

    def mix(m):
        for g in range(m * per_chunk, (m + 1) * per_chunk):
            ls = slice(g * LANES, (g + 1) * LANES)
            at = [(g - m * per_chunk) * dests + s for s in range(dests)]
            a = jnp.concatenate([orcv[rel(m), d, first] for d in at], axis=0).astype(F32)
            b = jnp.concatenate([orcv[rel(m + own), half - 1 - d, second] for d in at], axis=0).astype(F32)
            if m < own:
                rest = [prcv[m, jnp.where(side == 1, d, half - 1 - d)] for d in at]
                rest = jnp.concatenate(rest, axis=0).astype(F32)
                a, b = jnp.where(side == 1, a + rest, a), jnp.where(side == 1, b, b + rest)
            mixed = qmix[0, ls, :] * a + qmix[1, ls, :] * b
            for s, (start, row) in enumerate(pieces[g * dests : (g + 1) * dests]):
                lo, hi = max(row, low), min(row + rows, low + cblk)
                to = 8 + start - low
                xf[0, to + lo : to + hi, :] = mixed[s * rows + lo - row : s * rows + hi - row]

    for i in range(own):
        m = i
        receive(m)
        transform((i, 0), [near[m, t, 0] for t in range(half)])
        octets(lambda at: block_sums(hown, 0, m * rows, 0, (i, 0), at, more=True))
        for t, y in enumerate(result(0)):
            psnd[m, t] = y
        each(0, lambda j: part_copy(m, j).start())
    for i in range(own):
        m = i
        transform((i, 1), [near[m, half - 1 - t, 1] for t in range(half)])
        all_far(m).wait_recv()
        transform((i, 2), [far[m, t] for t in range(half)])

        def both(at):
            block_sums(hown, 0, m * rows, 0, (i, 0), at)
            block_sums(hown, 1, m * rows, 1, (i, 1), at, back=(i, 2))

        octets(both)
        send_back(m)
    for o in range(1, parts):
        filter_across(o, lax.rem(grp + parts - o, parts)).wait_recv()
    spectra(hother, [other[g] for g in range(parts)])
    for i in range(own):
        m = i
        receive(own + m)
        transform((0, 0), [near[own + m, t, 0] for t in range(half)])
        transform((0, 1), [near[own + m, half - 1 - t, 1] for t in range(half)])

        def both(at):
            block_sums(hother, 0, m * rows, 0, (0, 0), at)
            block_sums(hother, 1, m * rows, 1, (0, 1), at)

        octets(both)
        send_back(own + m)
    for i in range(own):
        all_back(i).wait_recv()
    for i in range(own):
        all_back(own + i).wait_recv()
        mix(own + i)
        all_part(i).wait_recv()
        mix(i)
    out[...] = xf[0, 8:held, :].astype(BF16)

    for m in range(nch):
        all_near(m).wait_send()
        all_back(m).wait_send()
    for i in range(own):
        all_far(i).wait_send()
        all_part(i).wait_send()
    filter_over().wait_send()
    for o in range(1, parts):
        filter_across(o, grp).wait_send()

    @pl.when(me < n - 1)
    def _():
        for a in range(3):
            halo(a, True).wait_send()

    @pl.when(me > 0)
    def _():
        for a in range(3):
            halo(a, False).wait_send()


def on_device(queries, key_rows, value_rows, short_taps, long_filter):
    n = lax.axis_size("ctx")
    parts = lax.axis_size("grp")
    channels, tokens = queries.shape
    cblk, length = long_filter.shape
    cpad, low, rows = dims_of(cblk)
    half = n // 2
    nch = 2 * cpad // rows
    own = nch // 2
    cp = n * cpad
    taps = jnp.swapaxes(short_taps, 1, 2)
    hbm = pl.BlockSpec(memory_space=pltpu.MemorySpace.HBM)
    vmem = pl.BlockSpec(memory_space=pltpu.VMEM)
    dma = pltpu.SemaphoreType.DMA
    return pl.pallas_call(
        functools.partial(kernel, n, parts, cblk),
        out_shape=jax.ShapeDtypeStruct((channels, tokens), BF16),
        in_specs=[hbm] * 7,
        out_specs=vmem,
        scratch_shapes=[
            pltpu.VMEM((3, channels, tokens), BF16),
            pltpu.VMEM((3, TAPS, channels), F32),
            pltpu.VMEM((cblk, length), BF16),
            pltpu.VMEM((parts, cblk, half * LANES // parts), BF16),
            dma((7,)),
            pltpu.VMEM((3, 8, cp), F32),
            pltpu.VMEM((2, 3, 8, cp), F32),
            pltpu.VMEM((3, channels + 24, LANES), F32),
            pltpu.VMEM((3, LANES + 16, cp), F32),
            pltpu.VMEM((2, cp, LANES), F32),
            pltpu.VMEM((2, LANES, cp), F32),
            pltpu.VMEM((nch, half, 2, rows, LANES), BF16),
            pltpu.VMEM((nch, half, 2, rows, LANES), BF16),
            pltpu.VMEM((own, half, rows, LANES), BF16),
            pltpu.VMEM((nch, half, 2, rows, LANES), BF16),
            pltpu.VMEM((nch, half, 2, rows, LANES), BF16),
            pltpu.VMEM((own, half, rows, LANES), BF16),
            pltpu.VMEM((own, half, rows, LANES), BF16),
            pltpu.VMEM((2, 2 * LANES, 2 * LANES), BF16),
            pltpu.VMEM((2, 2, 2 * LANES, LANES), BF16),
            pltpu.VMEM((2, n, cpad, 2 * LANES), F32),
            pltpu.VMEM((2, half, cpad, 2 * LANES), F32),
            pltpu.VMEM((own, 3, half, rows, 2 * LANES), F32),
            pltpu.VMEM((2, half, rows, 2 * LANES), F32),
            dma((2, 3)),
            dma((2, 3)),
            dma((nch,)),
            dma((nch,)),
            dma((own,)),
            dma((own,)),
            dma((nch,)),
            dma((nch,)),
            dma((own,)),
            dma((own,)),
            dma(()),
            dma(()),
            dma((parts,)),
            dma((parts,)),
        ],
        compiler_params=pltpu.CompilerParams(
            collective_id=0, has_side_effects=True, vmem_limit_bytes=62 * 1024 * 1024
        ),
    )(queries, key_rows, value_rows, taps, long_filter, *(jnp.asarray(x) for x in dft_tables()))


def solution(mesh):
    placed = (
        P(None, ("grp", "ctx")),
        P(None, ("grp", "ctx")),
        P(None, ("grp", "ctx")),
        P(),
        P("ctx", None),
    )
    return jax.shard_map(
        on_device, mesh=mesh, in_specs=placed, out_specs=P(None, ("grp", "ctx")), check_vma=False
    )
```

```python
import functools

import jax
import jax.numpy as jnp
import numpy as np
from jax import lax
from jax.experimental import pallas as pl
from jax.experimental.pallas import tpu as pltpu
from jax.sharding import PartitionSpec as P

TAPS = 7
LANES = 128
SHARES = 4
F32 = jnp.float32
BF16 = jnp.bfloat16


def dims_of(cblk):
    cpad = -(-cblk // 16) * 16
    low = (cpad - cblk) // 2
    even = 2 * low + cblk == cpad
    rows = 32 if even and cpad % 32 == 0 else cpad
    return cpad, low, rows


def unit(flip):
    i = lax.broadcasted_iota(jnp.int32, (LANES, LANES), 0)
    j = lax.broadcasted_iota(jnp.int32, (LANES, LANES), 1)
    j = LANES - 1 - j if flip else j
    return (i == j).astype(F32).astype(BF16)


def dft_tables():
    t = np.arange(2 * LANES)[:, None]
    angle = np.pi * t * (np.arange(LANES)[None] + 0.5) / LANES
    fwd = np.concatenate([np.cos(angle), -np.sin(angle)], axis=1)
    inv = fwd[LANES:].T / LANES

    def pair(x):
        high = x.astype(BF16)
        return np.stack([high, (x - high.astype(np.float64)).astype(BF16)])

    return pair(fwd), np.stack([pair(inv), pair(inv[:, ::-1])])


def mm(a, b):
    return lax.dot_general(a, b, (((1,), (0,)), ((), ())), preferred_element_type=F32)


def to_time_major(mat, x):
    return lax.dot_general(mat, x, (((1,), (1,)), ((), ())), preferred_element_type=F32)


def to_channel_major(x, mat):
    return lax.dot_general(x, mat, (((0,), (0,)), ((), ())), preferred_element_type=F32)


def short_sum(xs, taps, way, which, lanes, row, count):
    total = None
    for j in range(TAPS):
        start = 8 + row - j if way == 0 else 8 + row + j
        term = taps[way, which, j : j + 1, lanes] * xs[which, start : start + count, lanes]
        total = term if total is None else total + term
    return total


def kernel(
    n, parts, cblk, q_hbm, k_hbm, v_hbm, taps_hbm, filt_hbm, fwd_hbm, inv_hbm, out,
    xin, tin, filt, other, in_sem, alt, taps, xf, xs, qmix, prod, snd, near, far, osnd, orcv, psnd, prcv,
    fwd, inv, hown, hother, xh, yh,
    hs_sem, hr_sem, s_sem, r_sem, fs_sem, fr_sem, os_sem, or_sem, ps_sem, pr_sem, zs_sem, zr_sem, xs_sem, xr_sem,
):
    cpad, low, rows = dims_of(cblk)
    half = n // 2
    nch = 2 * cpad // rows
    cp = n * cpad
    groups = cp // LANES
    per_chunk = groups // nch
    dests = LANES // rows
    own = nch // 2
    span = other.shape[-1]
    channels = n * cblk
    held = 8 + channels
    me = lax.axis_index("ctx")
    grp = lax.axis_index("grp")
    side = me // half
    r = lax.rem(me, half)
    slot = jnp.where(side == 0, r, half - 1 - r)
    home = side * half
    away = (1 - side) * half

    loads = [
        pltpu.make_async_copy(src, dst, in_sem.at[i])
        for i, (src, dst) in enumerate((
            (q_hbm, xin.at[0]), (k_hbm, xin.at[1]), (v_hbm, xin.at[2]),
            (taps_hbm, tin), (fwd_hbm, fwd), (inv_hbm, inv), (filt_hbm, filt),
        ))
    ]
    for i in (1, 2, 3, 0, 4, 5, 6):
        loads[i].start()

    barrier = pltpu.get_barrier_semaphore()

    def greet(o, carry):
        pl.semaphore_signal(barrier, inc=1, device_id={"ctx": lax.rem(me + o, n)})
        return carry

    lax.fori_loop(1, n, greet, 0)
    for o in range(1, parts):
        pl.semaphore_signal(barrier, inc=1, device_id={"grp": lax.rem(grp + o, parts)})

    eye = unit(False)
    flip = unit(True)
    taps[...] = jnp.zeros((2, 3, 8, cp), F32)
    alt[...] = jnp.zeros((3, 8, cp), F32)
    for a in range(3):
        xf[a, 0:8, :] = jnp.zeros((8, LANES), F32)
        xf[a, held : held + 16, :] = jnp.zeros((16, LANES), F32)

    @pl.when(me == 0)
    def _():
        xs[:, 0:8, :] = jnp.zeros((3, 8, cp), F32)

    @pl.when(me == n - 1)
    def _():
        xs[:, 8 + LANES : 16 + LANES, :] = jnp.zeros((3, 8, cp), F32)

    pieces = [
        ((d + half * (at // cpad)) * cblk, at % cpad) for at in range(0, 2 * cpad, rows) for d in range(half)
    ]

    def turn(a):
        loads[a].wait()
        xf[a, 8:held, :] = xin[a].astype(F32)
        for g in range(groups):
            starts = [8 + first - low + at for first, at in pieces[g * dests : (g + 1) * dests]]
            block = jnp.concatenate([xf[a, i : i + rows, :] for i in starts], axis=0).astype(BF16)
            xs[a, 8 : 8 + LANES, g * LANES : (g + 1) * LANES] = to_time_major(eye, block)

    def halo(a, up):
        if up:
            return pltpu.make_async_remote_copy(
                src_ref=xs.at[a, pl.ds(LANES, 8)], dst_ref=xs.at[a, pl.ds(0, 8)],
                send_sem=hs_sem.at[0, a], recv_sem=hr_sem.at[0, a],
                device_id={"ctx": lax.rem(me + 1, n)},
            )
        return pltpu.make_async_remote_copy(
            src_ref=xs.at[a, pl.ds(8, 8)], dst_ref=xs.at[a, pl.ds(8 + LANES, 8)],
            send_sem=hs_sem.at[1, a], recv_sem=hr_sem.at[1, a],
            device_id={"ctx": lax.rem(me + n - 1, n)},
        )

    def halo_wait(arrays):
        @pl.when(me > 0)
        def _():
            for a in arrays:
                halo(a, True).wait_recv()

        @pl.when(me < n - 1)
        def _():
            for a in arrays:
                halo(a, False).wait_recv()

    def halo_start(arrays):
        @pl.when(me < n - 1)
        def _():
            for a in arrays:
                halo(a, True).start()

        @pl.when(me > 0)
        def _():
            for a in arrays:
                halo(a, False).start()

    def filter_over():
        return pltpu.make_async_remote_copy(
            src_ref=filt_hbm.at[:, pl.ds(pl.multiple_of(grp * span, LANES), span)], dst_ref=other.at[grp],
            send_sem=zs_sem, recv_sem=zr_sem, device_id={"ctx": away + r},
        )

    def filter_across(o, share):
        return pltpu.make_async_remote_copy(
            src_ref=other.at[share], dst_ref=other.at[share], send_sem=xs_sem.at[o], recv_sem=xr_sem.at[o],
            device_id={"grp": lax.rem(grp + o, parts)},
        )

    pl.semaphore_wait(barrier, n - 1 + parts - 1)
    filter_over().start()
    turn(1)
    turn(2)
    halo_start((1, 2))
    loads[3].wait()
    for ref, shift in ((taps.at[0], low), (alt, cpad - cblk - low)):
        for b, (first, row) in enumerate(pieces):
            base = first - shift + row
            lo, hi = max(base, 0), min(base + rows, channels)
            at = b * rows + lo - base
            ref[:, 0:TAPS, at : at + hi - lo] = tin[:, :, lo:hi]
    turner = unit(True).astype(F32)
    for g in range(groups):
        source = alt[:, :, cp - (g + 1) * LANES : cp - g * LANES].reshape(24, LANES)
        taps[1, :, :, g * LANES : (g + 1) * LANES] = jnp.dot(
            source, turner, precision=lax.Precision.HIGHEST, preferred_element_type=F32
        ).reshape(3, 8, LANES)

    def product(g, row, count, way):
        ls = slice(g * LANES, (g + 1) * LANES)
        prod[way, row : row + count, ls] = short_sum(xs, taps, way, 1, ls, row, count) * short_sum(
            xs, taps, way, 2, ls, row, count
        )

    for g in [*range(groups // 2, groups), *range(groups // 2)]:
        product(g, 8, LANES - 8, 0)
        product(g, 0, LANES - 8, 1)

    turn(0)
    halo_start((0,))
    def rel(m):
        return lax.rem(m + side * own, nch)

    first, second = side, 1 - side

    def near_copy(m, j):
        return pltpu.make_async_remote_copy(
            src_ref=snd.at[m, j], dst_ref=near.at[m, slot],
            send_sem=s_sem.at[m], recv_sem=r_sem.at[m], device_id={"ctx": home + j},
        )

    def far_copy(i, j):
        return pltpu.make_async_remote_copy(
            src_ref=snd.at[own + i, j, 0], dst_ref=far.at[i, slot],
            send_sem=fs_sem.at[i], recv_sem=fr_sem.at[i], device_id={"ctx": away + j},
        )

    def place_of(j):
        return jnp.where(side == 0, j, half - 1 - j)

    def back_copy(m, j):
        return pltpu.make_async_remote_copy(
            src_ref=osnd.at[m, place_of(j)], dst_ref=orcv.at[m, r],
            send_sem=os_sem.at[m], recv_sem=or_sem.at[m], device_id={"ctx": home + j},
        )

    def part_copy(i, j):
        return pltpu.make_async_remote_copy(
            src_ref=psnd.at[i, place_of(j)], dst_ref=prcv.at[i, r],
            send_sem=ps_sem.at[i], recv_sem=pr_sem.at[i], device_id={"ctx": away + j},
        )

    def all_of(src, dst, send_sem, recv_sem):
        return pltpu.make_async_remote_copy(
            src_ref=src, dst_ref=dst, send_sem=send_sem, recv_sem=recv_sem,
            device_id={"ctx": lax.rem(me + 1, n)},
        )

    def all_near(m):
        some = pl.ds(0, half - 1)
        return all_of(snd.at[m, some], near.at[m, some], s_sem.at[m], r_sem.at[m])

    def all_far(i):
        return all_of(far.at[i], far.at[i], fs_sem.at[i], fr_sem.at[i])

    def all_part(i):
        return all_of(psnd.at[i], prcv.at[i], ps_sem.at[i], pr_sem.at[i])

    def all_back(m):
        some = pl.ds(0, half - 1)
        return all_of(osnd.at[m, some], orcv.at[m, some], os_sem.at[m], or_sem.at[m])

    def each(first, act):
        def step(o, carry):
            act(lax.rem(r + o, half))
            return carry

        lax.fori_loop(first, half, step, 0, unroll=True if half <= 8 else 1)

    halo_wait((1, 2))
    for i in range(own):
        for m in (i, own + i):
            for g in range(m * per_chunk, (m + 1) * per_chunk):
                ls = slice(g * LANES, (g + 1) * LANES)
                product(g, 0, 8, 0)
                product(g, LANES - 8, 8, 1)
                pa = to_channel_major(prod[0, :, ls].astype(BF16), eye).astype(BF16)
                pb = to_channel_major(prod[1, :, ls].astype(BF16), flip).astype(BF16)
                at = (g - m * per_chunk) * dests
                for s in range(dests):
                    piece = slice(s * rows, (s + 1) * rows)
                    snd[rel(m), at + s, first] = pa[piece]
                    snd[rel(m + own), half - 1 - at - s, second] = pb[piece]
        each(1, lambda j: near_copy(i, j).start())
    for i in range(own):
        each(0, lambda j: far_copy(i, j).start())
    for i in range(own):
        each(1, lambda j: near_copy(own + i, j).start())

    halo_wait((0,))
    for g in range(groups):
        ls = slice(g * LANES, (g + 1) * LANES)
        for way in range(2):
            q = short_sum(xs, taps, way, 0, ls, 0, LANES)
            high = q.astype(BF16)
            rest = (q - high.astype(F32)).astype(BF16)
            qmix[way, ls, :] = to_channel_major(high, eye) + to_channel_major(rest, eye)

    for i in (4, 5, 6):
        loads[i].wait()
    row = lax.broadcasted_iota(jnp.int32, (cpad, cblk), 0)
    col = lax.broadcasted_iota(jnp.int32, (cpad, cblk), 1)
    places = [
        (row == jnp.where(side == of, low + col, low + cblk - 1 - col)).astype(F32).astype(BF16) for of in range(2)
    ]

    def spectra(dst, shares):
        for which, place in enumerate(places):
            lag = [jnp.zeros((cpad, LANES), BF16)]
            for share in shares:
                padded = mm(place, share).astype(BF16)
                lag += [padded[:, at : at + LANES] for at in range(0, share.shape[-1], LANES)]
            for d in range(len(lag) - 1):
                line = jnp.concatenate([lag[d], lag[d + 1]], axis=1)
                dst[which, d] = mm(line, fwd[0]) + mm(line, fwd[1])

    spectra(hown, [filt[...]])
    filter_over().wait_recv()
    for o in range(1, parts):
        filter_across(o, grp).start()

    re, im = slice(0, LANES), slice(LANES, 2 * LANES)

    def pair(ref, *index):
        return ref[(*index, re)], ref[(*index, im)]

    def times(x, h):
        return x[0] * h[0] - x[1] * h[1], x[0] * h[1] + x[1] * h[0]

    def block_sums(spec, kind, top, out_at, x_at, at, back=None, more=None):
        rs = pl.ds(at, 8)
        hs = pl.ds(top + at, 8)
        ahead, behind = (x_at, back) if more is None else (None, x_at)
        if half > 8:
            def output(t, carry):
                def term(seq, shift, d, total):
                    y = times(pair(xh, *seq, t + shift - d, rs), pair(spec, kind, d, hs))
                    return total[0] + y[0], total[1] + y[1]

                total = (jnp.zeros((8, LANES), F32),) * 2
                if ahead is not None:
                    total = lax.fori_loop(0, t + 1, functools.partial(term, ahead, 0), total)
                if behind is not None:
                    total = lax.fori_loop(t + 1, t + half + 1, functools.partial(term, behind, half), total)
                yh[out_at, t, rs, re], yh[out_at, t, rs, im] = total
                return carry

            lax.fori_loop(0, half, output, 0)
            return
        x = {}
        if behind is not None:
            x.update({t: pair(xh, *behind, t, rs) for t in range(half)})
        if ahead is not None:
            x.update({half + t: pair(xh, *ahead, t, rs) for t in range(half)})
        tile = 4
        for t0 in range(half, 2 * half, tile):
            acc = [None] * tile
            for d in range(2 * half):
                used = [u for u in range(tile) if t0 + u - d in x]
                if not used:
                    continue
                h = pair(spec, kind, d, hs)
                for u in used:
                    y = times(x[t0 + u - d], h)
                    acc[u] = y if acc[u] is None else (acc[u][0] + y[0], acc[u][1] + y[1])
            for u in range(tile):
                t = t0 - half + u
                yh[out_at, t, rs, re], yh[out_at, t, rs, im] = acc[u]

    def transform(dst, blocks):
        x = jnp.concatenate(blocks, axis=0)
        spec = mm(x, fwd[0, 0:LANES, :]) + mm(x, fwd[1, 0:LANES, :])
        xh[dst] = spec.reshape(half, rows, 2 * LANES)

    def result(which):
        y = yh[which].reshape(half * rows, 2 * LANES)
        high = y.astype(BF16)
        rest = (y - high.astype(F32)).astype(BF16)
        way = first if which == 0 else second
        y = (mm(high, inv[way, 0]) + mm(high, inv[way, 1]) + mm(rest, inv[way, 0])).astype(BF16)
        return [y[t * rows : (t + 1) * rows] for t in range(half)]

    def octets(body):
        def step(i, carry):
            body(pl.multiple_of(i * 8, 8))
            return carry

        lax.fori_loop(0, rows // 8, step, 0)

    def receive(m):
        all_near(m).wait_recv()
        near[m, slot] = snd[m, r]

    def send_back(m):
        for t, y in enumerate(result(0)):
            osnd[m, t, 0] = y
        for t, y in enumerate(result(1)):
            osnd[m, half - 1 - t, 1] = y
        each(1, lambda j: back_copy(m, j).start())
        orcv[m, r] = osnd[m, slot]

    def mix(m):
        for g in range(m * per_chunk, (m + 1) * per_chunk):
            ls = slice(g * LANES, (g + 1) * LANES)
            at = [(g - m * per_chunk) * dests + s for s in range(dests)]
            a = jnp.concatenate([orcv[rel(m), d, first] for d in at], axis=0).astype(F32)
            b = jnp.concatenate([orcv[rel(m + own), half - 1 - d, second] for d in at], axis=0).astype(F32)
            if m < own:
                rest = [prcv[m, jnp.where(side == 1, d, half - 1 - d)] for d in at]
                rest = jnp.concatenate(rest, axis=0).astype(F32)
                a, b = jnp.where(side == 1, a + rest, a), jnp.where(side == 1, b, b + rest)
            mixed = qmix[0, ls, :] * a + qmix[1, ls, :] * b
            for s, (start, row) in enumerate(pieces[g * dests : (g + 1) * dests]):
                lo, hi = max(row, low), min(row + rows, low + cblk)
                to = 8 + start - low
                xf[0, to + lo : to + hi, :] = mixed[s * rows + lo - row : s * rows + hi - row]

    for i in range(own):
        m = i
        receive(m)
        transform((i, 0), [near[m, t, 0] for t in range(half)])
        octets(lambda at: block_sums(hown, 0, m * rows, 0, (i, 0), at, more=True))
        for t, y in enumerate(result(0)):
            psnd[m, t] = y
        each(0, lambda j: part_copy(m, j).start())
    for i in range(own):
        m = i
        transform((i, 1), [near[m, half - 1 - t, 1] for t in range(half)])
        all_far(m).wait_recv()
        transform((i, 2), [far[m, t] for t in range(half)])

        def both(at):
            block_sums(hown, 0, m * rows, 0, (i, 0), at)
            block_sums(hown, 1, m * rows, 1, (i, 1), at, back=(i, 2))

        octets(both)
        send_back(m)
    for o in range(1, parts):
        filter_across(o, lax.rem(grp + parts - o, parts)).wait_recv()
    spectra(hother, [other[g] for g in range(parts)])
    for i in range(own):
        m = i
        receive(own + m)
        transform((0, 0), [near[own + m, t, 0] for t in range(half)])
        transform((0, 1), [near[own + m, half - 1 - t, 1] for t in range(half)])

        def both(at):
            block_sums(hother, 0, m * rows, 0, (0, 0), at)
            block_sums(hother, 1, m * rows, 1, (0, 1), at)

        octets(both)
        send_back(own + m)
    for i in range(own):
        all_back(i).wait_recv()
    for i in range(own):
        all_back(own + i).wait_recv()
        mix(own + i)
        all_part(i).wait_recv()
        mix(i)
    out[...] = xf[0, 8:held, :].astype(BF16)

    for m in range(nch):
        all_near(m).wait_send()
        all_back(m).wait_send()
    for i in range(own):
        all_far(i).wait_send()
        all_part(i).wait_send()
    filter_over().wait_send()
    for o in range(1, parts):
        filter_across(o, grp).wait_send()

    @pl.when(me < n - 1)
    def _():
        for a in range(3):
            halo(a, True).wait_send()

    @pl.when(me > 0)
    def _():
        for a in range(3):
            halo(a, False).wait_send()


def hand_on(src, dst, held, in_sem, out_sem):
    size = src.shape[0] // SHARES
    rows = [pl.ds(i * size, size) for i in range(SHARES)]
    into = [pltpu.make_async_copy(src.at[r], held.at[r], in_sem.at[i]) for i, r in enumerate(rows)]
    away = [pltpu.make_async_copy(held.at[r], dst.at[r], out_sem.at[i]) for i, r in enumerate(rows)]
    for copy in into:
        copy.start()
    for one, other in zip(into, away):
        one.wait()
        other.start()
    for copy in away:
        copy.wait()


def on_device(queries, key_rows, value_rows, short_taps, long_filter):
    n = lax.axis_size("ctx")
    parts = lax.axis_size("grp")
    channels, tokens = queries.shape
    cblk, length = long_filter.shape
    cpad, low, rows = dims_of(cblk)
    half = n // 2
    nch = 2 * cpad // rows
    own = nch // 2
    cp = n * cpad
    taps = jnp.swapaxes(short_taps, 1, 2)
    hbm = pl.BlockSpec(memory_space=pltpu.MemorySpace.HBM)
    vmem = pl.BlockSpec(memory_space=pltpu.VMEM)
    dma = pltpu.SemaphoreType.DMA
    mixed = pl.pallas_call(
        functools.partial(kernel, n, parts, cblk),
        out_shape=jax.ShapeDtypeStruct((channels, tokens), BF16),
        in_specs=[hbm] * 7,
        out_specs=vmem,
        scratch_shapes=[
            pltpu.VMEM((3, channels, tokens), BF16),
            pltpu.VMEM((3, TAPS, channels), F32),
            pltpu.VMEM((cblk, length), BF16),
            pltpu.VMEM((parts, cblk, half * LANES // parts), BF16),
            dma((7,)),
            pltpu.VMEM((3, 8, cp), F32),
            pltpu.VMEM((2, 3, 8, cp), F32),
            pltpu.VMEM((3, channels + 24, LANES), F32),
            pltpu.VMEM((3, LANES + 16, cp), F32),
            pltpu.VMEM((2, cp, LANES), F32),
            pltpu.VMEM((2, LANES, cp), F32),
            pltpu.VMEM((nch, half, 2, rows, LANES), BF16),
            pltpu.VMEM((nch, half, 2, rows, LANES), BF16),
            pltpu.VMEM((own, half, rows, LANES), BF16),
            pltpu.VMEM((nch, half, 2, rows, LANES), BF16),
            pltpu.VMEM((nch, half, 2, rows, LANES), BF16),
            pltpu.VMEM((own, half, rows, LANES), BF16),
            pltpu.VMEM((own, half, rows, LANES), BF16),
            pltpu.VMEM((2, 2 * LANES, 2 * LANES), BF16),
            pltpu.VMEM((2, 2, 2 * LANES, LANES), BF16),
            pltpu.VMEM((2, n, cpad, 2 * LANES), F32),
            pltpu.VMEM((2, half, cpad, 2 * LANES), F32),
            pltpu.VMEM((own, 3, half, rows, 2 * LANES), F32),
            pltpu.VMEM((2, half, rows, 2 * LANES), F32),
            dma((2, 3)),
            dma((2, 3)),
            dma((nch,)),
            dma((nch,)),
            dma((own,)),
            dma((own,)),
            dma((nch,)),
            dma((nch,)),
            dma((own,)),
            dma((own,)),
            dma(()),
            dma(()),
            dma((parts,)),
            dma((parts,)),
        ],
        compiler_params=pltpu.CompilerParams(
            collective_id=0, has_side_effects=True, vmem_limit_bytes=62 * 1024 * 1024
        ),
    )(queries, key_rows, value_rows, taps, long_filter, *(jnp.asarray(x) for x in dft_tables()))
    return pl.pallas_call(
        hand_on,
        out_shape=jax.ShapeDtypeStruct((channels, tokens), BF16),
        in_specs=[hbm],
        out_specs=hbm,
        scratch_shapes=[pltpu.VMEM((channels, tokens), BF16), dma((SHARES,)), dma((SHARES,))],
    )(mixed)


def solution(mesh):
    placed = (
        P(None, ("grp", "ctx")),
        P(None, ("grp", "ctx")),
        P(None, ("grp", "ctx")),
        P(),
        P("ctx", None),
    )
    return jax.shard_map(
        on_device, mesh=mesh, in_specs=placed, out_specs=P(None, ("grp", "ctx")), check_vma=False
    )
```

```python
import functools

import jax
import jax.numpy as jnp
import numpy as np
from jax import lax
from jax.experimental import pallas as pl
from jax.experimental.pallas import tpu as pltpu
from jax.sharding import PartitionSpec as P

TAPS = 7
LANES = 128
SHARES = 4
F32 = jnp.float32
BF16 = jnp.bfloat16


def dims_of(cblk):
    cpad = -(-cblk // 16) * 16
    low = (cpad - cblk) // 2
    even = 2 * low + cblk == cpad
    rows = 32 if even and cpad % 32 == 0 else cpad
    return cpad, low, rows


def unit(flip):
    i = lax.broadcasted_iota(jnp.int32, (LANES, LANES), 0)
    j = lax.broadcasted_iota(jnp.int32, (LANES, LANES), 1)
    j = LANES - 1 - j if flip else j
    return (i == j).astype(F32).astype(BF16)


def dft_tables():
    t = np.arange(2 * LANES)[:, None]
    angle = np.pi * t * (np.arange(LANES)[None] + 0.5) / LANES
    fwd = np.concatenate([np.cos(angle), -np.sin(angle)], axis=1)
    inv = fwd[LANES:].T / LANES

    def pair(x):
        high = x.astype(BF16)
        return np.stack([high, (x - high.astype(np.float64)).astype(BF16)])

    return pair(fwd), np.stack([pair(inv), pair(inv[:, ::-1])])


def mm(a, b):
    return lax.dot_general(a, b, (((1,), (0,)), ((), ())), preferred_element_type=F32)


def to_time_major(mat, x):
    return lax.dot_general(mat, x, (((1,), (1,)), ((), ())), preferred_element_type=F32)


def to_channel_major(x, mat):
    return lax.dot_general(x, mat, (((0,), (0,)), ((), ())), preferred_element_type=F32)


def short_sum(xs, taps, way, which, lanes, row, count):
    total = None
    for j in range(TAPS):
        start = 8 + row - j if way == 0 else 8 + row + j
        term = taps[way, which, j : j + 1, lanes] * xs[which, start : start + count, lanes]
        total = term if total is None else total + term
    return total


def kernel(
    n, parts, cblk, q_hbm, k_hbm, v_hbm, taps_hbm, filt_hbm, fwd_hbm, inv_hbm, out,
    xin, tin, filt, other, in_sem, alt, taps, xf, xs, qmix, prod, snd, near, far, osnd, orcv, psnd, prcv,
    fwd, inv, hown, hother, xh, yh,
    hs_sem, hr_sem, s_sem, r_sem, fs_sem, fr_sem, os_sem, or_sem, ps_sem, pr_sem, zs_sem, zr_sem, xs_sem, xr_sem,
):
    cpad, low, rows = dims_of(cblk)
    half = n // 2
    nch = 2 * cpad // rows
    cp = n * cpad
    groups = cp // LANES
    per_chunk = groups // nch
    dests = LANES // rows
    own = nch // 2
    span = other.shape[-1]
    channels = n * cblk
    held = 8 + channels
    me = lax.axis_index("ctx")
    grp = lax.axis_index("grp")
    side = me // half
    r = lax.rem(me, half)
    slot = jnp.where(side == 0, r, half - 1 - r)
    home = side * half
    away = (1 - side) * half

    loads = [
        pltpu.make_async_copy(src, dst, in_sem.at[i])
        for i, (src, dst) in enumerate((
            (q_hbm, xin.at[0]), (k_hbm, xin.at[1]), (v_hbm, xin.at[2]),
            (taps_hbm, tin), (fwd_hbm, fwd), (inv_hbm, inv), (filt_hbm, filt),
        ))
    ]
    for i in (1, 2):
        loads[i].start()

    barrier = pltpu.get_barrier_semaphore()

    def greet(o, carry):
        pl.semaphore_signal(barrier, inc=1, device_id={"ctx": lax.rem(me + o, n)})
        return carry

    lax.fori_loop(1, n, greet, 0)
    for o in range(1, parts):
        pl.semaphore_signal(barrier, inc=1, device_id={"grp": lax.rem(grp + o, parts)})

    for i in (3, 0):
        loads[i].start()

    eye = unit(False)
    flip = unit(True)
    taps[...] = jnp.zeros((2, 3, 8, cp), F32)
    alt[...] = jnp.zeros((3, 8, cp), F32)
    for a in range(3):
        xf[a, 0:8, :] = jnp.zeros((8, LANES), F32)
        xf[a, held : held + 16, :] = jnp.zeros((16, LANES), F32)

    @pl.when(me == 0)
    def _():
        xs[:, 0:8, :] = jnp.zeros((3, 8, cp), F32)

    @pl.when(me == n - 1)
    def _():
        xs[:, 8 + LANES : 16 + LANES, :] = jnp.zeros((3, 8, cp), F32)

    pieces = [
        ((d + half * (at // cpad)) * cblk, at % cpad) for at in range(0, 2 * cpad, rows) for d in range(half)
    ]

    def turn(a):
        loads[a].wait()
        xf[a, 8:held, :] = xin[a].astype(F32)
        for g in range(groups):
            starts = [8 + first - low + at for first, at in pieces[g * dests : (g + 1) * dests]]
            block = jnp.concatenate([xf[a, i : i + rows, :] for i in starts], axis=0).astype(BF16)
            xs[a, 8 : 8 + LANES, g * LANES : (g + 1) * LANES] = to_time_major(eye, block)

    def halo(a, up):
        if up:
            return pltpu.make_async_remote_copy(
                src_ref=xs.at[a, pl.ds(LANES, 8)], dst_ref=xs.at[a, pl.ds(0, 8)],
                send_sem=hs_sem.at[0, a], recv_sem=hr_sem.at[0, a],
                device_id={"ctx": lax.rem(me + 1, n)},
            )
        return pltpu.make_async_remote_copy(
            src_ref=xs.at[a, pl.ds(8, 8)], dst_ref=xs.at[a, pl.ds(8 + LANES, 8)],
            send_sem=hs_sem.at[1, a], recv_sem=hr_sem.at[1, a],
            device_id={"ctx": lax.rem(me + n - 1, n)},
        )

    def halo_wait(arrays):
        @pl.when(me > 0)
        def _():
            for a in arrays:
                halo(a, True).wait_recv()

        @pl.when(me < n - 1)
        def _():
            for a in arrays:
                halo(a, False).wait_recv()

    def halo_start(arrays):
        @pl.when(me < n - 1)
        def _():
            for a in arrays:
                halo(a, True).start()

        @pl.when(me > 0)
        def _():
            for a in arrays:
                halo(a, False).start()

    def filter_over():
        return pltpu.make_async_remote_copy(
            src_ref=filt_hbm.at[:, pl.ds(pl.multiple_of(grp * span, LANES), span)], dst_ref=other.at[grp],
            send_sem=zs_sem, recv_sem=zr_sem, device_id={"ctx": away + r},
        )

    def filter_across(o, share):
        return pltpu.make_async_remote_copy(
            src_ref=other.at[share], dst_ref=other.at[share], send_sem=xs_sem.at[o], recv_sem=xr_sem.at[o],
            device_id={"grp": lax.rem(grp + o, parts)},
        )

    pl.semaphore_wait(barrier, n - 1 + parts - 1)
    filter_over().start()
    turn(1)
    halo_start((1,))
    turn(2)
    halo_start((2,))
    for i in (4, 5, 6):
        loads[i].start()
    loads[3].wait()
    for ref, shift in ((taps.at[0], low), (alt, cpad - cblk - low)):
        for b, (first, row) in enumerate(pieces):
            base = first - shift + row
            lo, hi = max(base, 0), min(base + rows, channels)
            at = b * rows + lo - base
            ref[:, 0:TAPS, at : at + hi - lo] = tin[:, :, lo:hi]
    turner = unit(True).astype(F32)
    for g in range(groups):
        source = alt[:, :, cp - (g + 1) * LANES : cp - g * LANES].reshape(24, LANES)
        taps[1, :, :, g * LANES : (g + 1) * LANES] = jnp.dot(
            source, turner, precision=lax.Precision.HIGHEST, preferred_element_type=F32
        ).reshape(3, 8, LANES)

    def product(g, row, count, way):
        ls = slice(g * LANES, (g + 1) * LANES)
        prod[way, row : row + count, ls] = short_sum(xs, taps, way, 1, ls, row, count) * short_sum(
            xs, taps, way, 2, ls, row, count
        )

    for g in [*range(groups // 2, groups), *range(groups // 2)]:
        product(g, 8, LANES - 8, 0)
        product(g, 0, LANES - 8, 1)

    turn(0)
    halo_start((0,))
    def rel(m):
        return lax.rem(m + side * own, nch)

    first, second = side, 1 - side

    def near_copy(m, j):
        return pltpu.make_async_remote_copy(
            src_ref=snd.at[m, j], dst_ref=near.at[m, slot],
            send_sem=s_sem.at[m], recv_sem=r_sem.at[m], device_id={"ctx": home + j},
        )

    def far_copy(i, j):
        return pltpu.make_async_remote_copy(
            src_ref=snd.at[own + i, j, 0], dst_ref=far.at[i, slot],
            send_sem=fs_sem.at[i], recv_sem=fr_sem.at[i], device_id={"ctx": away + j},
        )

    def place_of(j):
        return jnp.where(side == 0, j, half - 1 - j)

    def back_copy(m, j):
        return pltpu.make_async_remote_copy(
            src_ref=osnd.at[m, place_of(j)], dst_ref=orcv.at[m, r],
            send_sem=os_sem.at[m], recv_sem=or_sem.at[m], device_id={"ctx": home + j},
        )

    def part_copy(i, j):
        return pltpu.make_async_remote_copy(
            src_ref=psnd.at[i, place_of(j)], dst_ref=prcv.at[i, r],
            send_sem=ps_sem.at[i], recv_sem=pr_sem.at[i], device_id={"ctx": away + j},
        )

    def all_of(src, dst, send_sem, recv_sem):
        return pltpu.make_async_remote_copy(
            src_ref=src, dst_ref=dst, send_sem=send_sem, recv_sem=recv_sem,
            device_id={"ctx": lax.rem(me + 1, n)},
        )

    def all_near(m):
        some = pl.ds(0, half - 1)
        return all_of(snd.at[m, some], near.at[m, some], s_sem.at[m], r_sem.at[m])

    def all_far(i):
        return all_of(far.at[i], far.at[i], fs_sem.at[i], fr_sem.at[i])

    def all_part(i):
        return all_of(psnd.at[i], prcv.at[i], ps_sem.at[i], pr_sem.at[i])

    def all_back(m):
        some = pl.ds(0, half - 1)
        return all_of(osnd.at[m, some], orcv.at[m, some], os_sem.at[m], or_sem.at[m])

    def each(first, act):
        def step(o, carry):
            act(lax.rem(r + o, half))
            return carry

        lax.fori_loop(first, half, step, 0, unroll=True if half <= 8 else 1)

    halo_wait((1, 2))
    for i in range(own):
        for m in (i, own + i):
            for g in range(m * per_chunk, (m + 1) * per_chunk):
                ls = slice(g * LANES, (g + 1) * LANES)
                product(g, 0, 8, 0)
                product(g, LANES - 8, 8, 1)
                pa = to_channel_major(prod[0, :, ls].astype(BF16), eye).astype(BF16)
                pb = to_channel_major(prod[1, :, ls].astype(BF16), flip).astype(BF16)
                at = (g - m * per_chunk) * dests
                for s in range(dests):
                    piece = slice(s * rows, (s + 1) * rows)
                    snd[rel(m), at + s, first] = pa[piece]
                    snd[rel(m + own), half - 1 - at - s, second] = pb[piece]
        each(1, lambda j: near_copy(i, j).start())
    for i in range(own):
        each(0, lambda j: far_copy(i, j).start())
    for i in range(own):
        each(1, lambda j: near_copy(own + i, j).start())

    halo_wait((0,))
    for g in range(groups):
        ls = slice(g * LANES, (g + 1) * LANES)
        for way in range(2):
            q = short_sum(xs, taps, way, 0, ls, 0, LANES)
            high = q.astype(BF16)
            rest = (q - high.astype(F32)).astype(BF16)
            qmix[way, ls, :] = to_channel_major(high, eye) + to_channel_major(rest, eye)

    for i in (4, 5, 6):
        loads[i].wait()
    row = lax.broadcasted_iota(jnp.int32, (cpad, cblk), 0)
    col = lax.broadcasted_iota(jnp.int32, (cpad, cblk), 1)
    places = [
        (row == jnp.where(side == of, low + col, low + cblk - 1 - col)).astype(F32).astype(BF16) for of in range(2)
    ]

    def spectra(dst, shares):
        for which, place in enumerate(places):
            lag = [jnp.zeros((cpad, LANES), BF16)]
            for share in shares:
                padded = mm(place, share).astype(BF16)
                lag += [padded[:, at : at + LANES] for at in range(0, share.shape[-1], LANES)]
            for d in range(len(lag) - 1):
                line = jnp.concatenate([lag[d], lag[d + 1]], axis=1)
                dst[which, d] = mm(line, fwd[0]) + mm(line, fwd[1])

    spectra(hown, [filt[...]])
    filter_over().wait_recv()
    for o in range(1, parts):
        filter_across(o, grp).start()

    re, im = slice(0, LANES), slice(LANES, 2 * LANES)

    def pair(ref, *index):
        return ref[(*index, re)], ref[(*index, im)]

    def times(x, h):
        return x[0] * h[0] - x[1] * h[1], x[0] * h[1] + x[1] * h[0]

    def block_sums(spec, kind, top, out_at, x_at, at, back=None, more=None):
        rs = pl.ds(at, 8)
        hs = pl.ds(top + at, 8)
        ahead, behind = (x_at, back) if more is None else (None, x_at)
        if half > 8:
            def output(t, carry):
                def term(seq, shift, d, total):
                    y = times(pair(xh, *seq, t + shift - d, rs), pair(spec, kind, d, hs))
                    return total[0] + y[0], total[1] + y[1]

                total = (jnp.zeros((8, LANES), F32),) * 2
                if ahead is not None:
                    total = lax.fori_loop(0, t + 1, functools.partial(term, ahead, 0), total)
                if behind is not None:
                    total = lax.fori_loop(t + 1, t + half + 1, functools.partial(term, behind, half), total)
                yh[out_at, t, rs, re], yh[out_at, t, rs, im] = total
                return carry

            lax.fori_loop(0, half, output, 0)
            return
        x = {}
        if behind is not None:
            x.update({t: pair(xh, *behind, t, rs) for t in range(half)})
        if ahead is not None:
            x.update({half + t: pair(xh, *ahead, t, rs) for t in range(half)})
        tile = 4
        for t0 in range(half, 2 * half, tile):
            acc = [None] * tile
            for d in range(2 * half):
                used = [u for u in range(tile) if t0 + u - d in x]
                if not used:
                    continue
                h = pair(spec, kind, d, hs)
                for u in used:
                    y = times(x[t0 + u - d], h)
                    acc[u] = y if acc[u] is None else (acc[u][0] + y[0], acc[u][1] + y[1])
            for u in range(tile):
                t = t0 - half + u
                yh[out_at, t, rs, re], yh[out_at, t, rs, im] = acc[u]

    def transform(dst, blocks):
        x = jnp.concatenate(blocks, axis=0)
        spec = mm(x, fwd[0, 0:LANES, :]) + mm(x, fwd[1, 0:LANES, :])
        xh[dst] = spec.reshape(half, rows, 2 * LANES)

    def result(which):
        y = yh[which].reshape(half * rows, 2 * LANES)
        high = y.astype(BF16)
        rest = (y - high.astype(F32)).astype(BF16)
        way = first if which == 0 else second
        y = (mm(high, inv[way, 0]) + mm(high, inv[way, 1]) + mm(rest, inv[way, 0])).astype(BF16)
        return [y[t * rows : (t + 1) * rows] for t in range(half)]

    def octets(body):
        def step(i, carry):
            body(pl.multiple_of(i * 8, 8))
            return carry

        lax.fori_loop(0, rows // 8, step, 0)

    def receive(m):
        all_near(m).wait_recv()
        near[m, slot] = snd[m, r]

    def send_back(m):
        for t, y in enumerate(result(0)):
            osnd[m, t, 0] = y
        for t, y in enumerate(result(1)):
            osnd[m, half - 1 - t, 1] = y
        each(1, lambda j: back_copy(m, j).start())
        orcv[m, r] = osnd[m, slot]

    def mix(m):
        for g in range(m * per_chunk, (m + 1) * per_chunk):
            ls = slice(g * LANES, (g + 1) * LANES)
            at = [(g - m * per_chunk) * dests + s for s in range(dests)]
            a = jnp.concatenate([orcv[rel(m), d, first] for d in at], axis=0).astype(F32)
            b = jnp.concatenate([orcv[rel(m + own), half - 1 - d, second] for d in at], axis=0).astype(F32)
            if m < own:
                rest = [prcv[m, jnp.where(side == 1, d, half - 1 - d)] for d in at]
                rest = jnp.concatenate(rest, axis=0).astype(F32)
                a, b = jnp.where(side == 1, a + rest, a), jnp.where(side == 1, b, b + rest)
            mixed = qmix[0, ls, :] * a + qmix[1, ls, :] * b
            for s, (start, row) in enumerate(pieces[g * dests : (g + 1) * dests]):
                lo, hi = max(row, low), min(row + rows, low + cblk)
                to = 8 + start - low
                xf[0, to + lo : to + hi, :] = mixed[s * rows + lo - row : s * rows + hi - row]

    for i in range(own):
        m = i
        receive(m)
        transform((i, 0), [near[m, t, 0] for t in range(half)])
        octets(lambda at: block_sums(hown, 0, m * rows, 0, (i, 0), at, more=True))
        for t, y in enumerate(result(0)):
            psnd[m, t] = y
        each(0, lambda j: part_copy(m, j).start())
    for i in range(own):
        m = i
        transform((i, 1), [near[m, half - 1 - t, 1] for t in range(half)])
        all_far(m).wait_recv()
        transform((i, 2), [far[m, t] for t in range(half)])

        def both(at):
            block_sums(hown, 0, m * rows, 0, (i, 0), at)
            block_sums(hown, 1, m * rows, 1, (i, 1), at, back=(i, 2))

        octets(both)
        send_back(m)
    for o in range(1, parts):
        filter_across(o, lax.rem(grp + parts - o, parts)).wait_recv()
    spectra(hother, [other[g] for g in range(parts)])
    for i in range(own):
        m = i
        receive(own + m)
        transform((0, 0), [near[own + m, t, 0] for t in range(half)])
        transform((0, 1), [near[own + m, half - 1 - t, 1] for t in range(half)])

        def both(at):
            block_sums(hother, 0, m * rows, 0, (0, 0), at)
            block_sums(hother, 1, m * rows, 1, (0, 1), at)

        octets(both)
        send_back(own + m)
    for i in range(own):
        all_back(i).wait_recv()
    for i in range(own):
        all_back(own + i).wait_recv()
        mix(own + i)
        all_part(i).wait_recv()
        mix(i)
    out[...] = xf[0, 8:held, :].astype(BF16)

    for m in range(nch):
        all_near(m).wait_send()
        all_back(m).wait_send()
    for i in range(own):
        all_far(i).wait_send()
        all_part(i).wait_send()
    filter_over().wait_send()
    for o in range(1, parts):
        filter_across(o, grp).wait_send()

    @pl.when(me < n - 1)
    def _():
        for a in range(3):
            halo(a, True).wait_send()

    @pl.when(me > 0)
    def _():
        for a in range(3):
            halo(a, False).wait_send()


def hand_on(src, dst, held, in_sem, out_sem):
    size = src.shape[0] // SHARES
    rows = [pl.ds(i * size, size) for i in range(SHARES)]
    into = [pltpu.make_async_copy(src.at[r], held.at[r], in_sem.at[i]) for i, r in enumerate(rows)]
    away = [pltpu.make_async_copy(held.at[r], dst.at[r], out_sem.at[i]) for i, r in enumerate(rows)]
    for copy in into:
        copy.start()
    for one, other in zip(into, away):
        one.wait()
        other.start()
    for copy in away:
        copy.wait()


def on_device(queries, key_rows, value_rows, short_taps, long_filter):
    n = lax.axis_size("ctx")
    parts = lax.axis_size("grp")
    channels, tokens = queries.shape
    cblk, length = long_filter.shape
    cpad, low, rows = dims_of(cblk)
    half = n // 2
    nch = 2 * cpad // rows
    own = nch // 2
    cp = n * cpad
    taps = jnp.swapaxes(short_taps, 1, 2)
    hbm = pl.BlockSpec(memory_space=pltpu.MemorySpace.HBM)
    vmem = pl.BlockSpec(memory_space=pltpu.VMEM)
    dma = pltpu.SemaphoreType.DMA
    mixed = pl.pallas_call(
        functools.partial(kernel, n, parts, cblk),
        out_shape=jax.ShapeDtypeStruct((channels, tokens), BF16),
        in_specs=[hbm] * 7,
        out_specs=vmem,
        scratch_shapes=[
            pltpu.VMEM((3, channels, tokens), BF16),
            pltpu.VMEM((3, TAPS, channels), F32),
            pltpu.VMEM((cblk, length), BF16),
            pltpu.VMEM((parts, cblk, half * LANES // parts), BF16),
            dma((7,)),
            pltpu.VMEM((3, 8, cp), F32),
            pltpu.VMEM((2, 3, 8, cp), F32),
            pltpu.VMEM((3, channels + 24, LANES), F32),
            pltpu.VMEM((3, LANES + 16, cp), F32),
            pltpu.VMEM((2, cp, LANES), F32),
            pltpu.VMEM((2, LANES, cp), F32),
            pltpu.VMEM((nch, half, 2, rows, LANES), BF16),
            pltpu.VMEM((nch, half, 2, rows, LANES), BF16),
            pltpu.VMEM((own, half, rows, LANES), BF16),
            pltpu.VMEM((nch, half, 2, rows, LANES), BF16),
            pltpu.VMEM((nch, half, 2, rows, LANES), BF16),
            pltpu.VMEM((own, half, rows, LANES), BF16),
            pltpu.VMEM((own, half, rows, LANES), BF16),
            pltpu.VMEM((2, 2 * LANES, 2 * LANES), BF16),
            pltpu.VMEM((2, 2, 2 * LANES, LANES), BF16),
            pltpu.VMEM((2, n, cpad, 2 * LANES), F32),
            pltpu.VMEM((2, half, cpad, 2 * LANES), F32),
            pltpu.VMEM((own, 3, half, rows, 2 * LANES), F32),
            pltpu.VMEM((2, half, rows, 2 * LANES), F32),
            dma((2, 3)),
            dma((2, 3)),
            dma((nch,)),
            dma((nch,)),
            dma((own,)),
            dma((own,)),
            dma((nch,)),
            dma((nch,)),
            dma((own,)),
            dma((own,)),
            dma(()),
            dma(()),
            dma((parts,)),
            dma((parts,)),
        ],
        compiler_params=pltpu.CompilerParams(
            collective_id=0, has_side_effects=True, vmem_limit_bytes=62 * 1024 * 1024
        ),
    )(queries, key_rows, value_rows, taps, long_filter, *(jnp.asarray(x) for x in dft_tables()))
    return pl.pallas_call(
        hand_on,
        out_shape=jax.ShapeDtypeStruct((channels, tokens), BF16),
        in_specs=[hbm],
        out_specs=hbm,
        scratch_shapes=[pltpu.VMEM((channels, tokens), BF16), dma((SHARES,)), dma((SHARES,))],
    )(mixed)


def solution(mesh):
    placed = (
        P(None, ("grp", "ctx")),
        P(None, ("grp", "ctx")),
        P(None, ("grp", "ctx")),
        P(),
        P("ctx", None),
    )
    return jax.shard_map(
        on_device, mesh=mesh, in_specs=placed, out_specs=P(None, ("grp", "ctx")), check_vma=False
    )
```

```python
import functools

import jax
import jax.numpy as jnp
import numpy as np
from jax import lax
from jax.experimental import pallas as pl
from jax.experimental.pallas import tpu as pltpu
from jax.sharding import PartitionSpec as P

TAPS = 7
LANES = 128
SHARES = 4
F32 = jnp.float32
BF16 = jnp.bfloat16


def dims_of(cblk):
    cpad = -(-cblk // 16) * 16
    low = (cpad - cblk) // 2
    even = 2 * low + cblk == cpad
    rows = 32 if even and cpad % 32 == 0 else cpad
    return cpad, low, rows


def unit(flip):
    i = lax.broadcasted_iota(jnp.int32, (LANES, LANES), 0)
    j = lax.broadcasted_iota(jnp.int32, (LANES, LANES), 1)
    j = LANES - 1 - j if flip else j
    return (i == j).astype(F32).astype(BF16)


def dft_tables():
    t = np.arange(2 * LANES)[:, None]
    angle = np.pi * t * (np.arange(LANES)[None] + 0.5) / LANES
    fwd = np.concatenate([np.cos(angle), -np.sin(angle)], axis=1)
    inv = fwd[LANES:].T / LANES

    def pair(x):
        high = x.astype(BF16)
        return np.stack([high, (x - high.astype(np.float64)).astype(BF16)])

    return pair(fwd), np.stack([np.concatenate(pair(x), axis=1) for x in (inv, inv[:, ::-1])])


def mm(a, b):
    return lax.dot_general(a, b, (((1,), (0,)), ((), ())), preferred_element_type=F32)


def to_time_major(mat, x):
    return lax.dot_general(mat, x, (((1,), (1,)), ((), ())), preferred_element_type=F32)


def to_channel_major(x, mat):
    return lax.dot_general(x, mat, (((0,), (0,)), ((), ())), preferred_element_type=F32)


def short_sum(xs, taps, way, which, lanes, row, count):
    total = None
    for j in range(TAPS):
        start = 8 + row - j if way == 0 else 8 + row + j
        term = taps[way, which, j : j + 1, lanes] * xs[which, start : start + count, lanes]
        total = term if total is None else total + term
    return total


def kernel(
    n, parts, cblk, q_hbm, k_hbm, v_hbm, taps_hbm, filt_hbm, fwd_hbm, inv_hbm, out,
    xin, tin, filt, other, in_sem, alt, taps, xf, xs, qmix, prod, snd, near, far, osnd, orcv, psnd, prcv,
    fwd, inv, hown, hother, xh, yh,
    hs_sem, hr_sem, s_sem, r_sem, fs_sem, fr_sem, os_sem, or_sem, ps_sem, pr_sem, zs_sem, zr_sem, xs_sem, xr_sem,
):
    cpad, low, rows = dims_of(cblk)
    half = n // 2
    nch = 2 * cpad // rows
    cp = n * cpad
    groups = cp // LANES
    per_chunk = groups // nch
    dests = LANES // rows
    own = nch // 2
    span = other.shape[-1]
    channels = n * cblk
    held = 8 + channels
    me = lax.axis_index("ctx")
    grp = lax.axis_index("grp")
    side = me // half
    r = lax.rem(me, half)
    slot = jnp.where(side == 0, r, half - 1 - r)
    home = side * half
    away = (1 - side) * half

    loads = [
        pltpu.make_async_copy(src, dst, in_sem.at[i])
        for i, (src, dst) in enumerate((
            (q_hbm, xin.at[0]), (k_hbm, xin.at[1]), (v_hbm, xin.at[2]),
            (taps_hbm, tin), (fwd_hbm, fwd), (inv_hbm, inv), (filt_hbm, filt),
        ))
    ]
    for i in (1, 2):
        loads[i].start()

    barrier = pltpu.get_barrier_semaphore()

    def greet(o, carry):
        pl.semaphore_signal(barrier, inc=1, device_id={"ctx": lax.rem(me + o, n)})
        return carry

    lax.fori_loop(1, n, greet, 0)
    for o in range(1, parts):
        pl.semaphore_signal(barrier, inc=1, device_id={"grp": lax.rem(grp + o, parts)})

    for i in (3, 0):
        loads[i].start()

    eye = unit(False)
    flip = unit(True)
    taps[...] = jnp.zeros((2, 3, 8, cp), F32)
    alt[...] = jnp.zeros((3, 8, cp), F32)
    for a in range(3):
        xf[a, 0:8, :] = jnp.zeros((8, LANES), F32)
        xf[a, held : held + 16, :] = jnp.zeros((16, LANES), F32)

    @pl.when(me == 0)
    def _():
        xs[:, 0:8, :] = jnp.zeros((3, 8, cp), F32)

    @pl.when(me == n - 1)
    def _():
        xs[:, 8 + LANES : 16 + LANES, :] = jnp.zeros((3, 8, cp), F32)

    pieces = [
        ((d + half * (at // cpad)) * cblk, at % cpad) for at in range(0, 2 * cpad, rows) for d in range(half)
    ]

    def turn(a):
        loads[a].wait()
        xf[a, 8:held, :] = xin[a].astype(F32)
        for g in range(groups):
            starts = [8 + first - low + at for first, at in pieces[g * dests : (g + 1) * dests]]
            block = jnp.concatenate([xf[a, i : i + rows, :] for i in starts], axis=0).astype(BF16)
            xs[a, 8 : 8 + LANES, g * LANES : (g + 1) * LANES] = to_time_major(eye, block)

    def halo(a, up):
        if up:
            return pltpu.make_async_remote_copy(
                src_ref=xs.at[a, pl.ds(LANES, 8)], dst_ref=xs.at[a, pl.ds(0, 8)],
                send_sem=hs_sem.at[0, a], recv_sem=hr_sem.at[0, a],
                device_id={"ctx": lax.rem(me + 1, n)},
            )
        return pltpu.make_async_remote_copy(
            src_ref=xs.at[a, pl.ds(8, 8)], dst_ref=xs.at[a, pl.ds(8 + LANES, 8)],
            send_sem=hs_sem.at[1, a], recv_sem=hr_sem.at[1, a],
            device_id={"ctx": lax.rem(me + n - 1, n)},
        )

    def halo_wait(arrays):
        @pl.when(me > 0)
        def _():
            for a in arrays:
                halo(a, True).wait_recv()

        @pl.when(me < n - 1)
        def _():
            for a in arrays:
                halo(a, False).wait_recv()

    def halo_start(arrays):
        @pl.when(me < n - 1)
        def _():
            for a in arrays:
                halo(a, True).start()

        @pl.when(me > 0)
        def _():
            for a in arrays:
                halo(a, False).start()

    def filter_over():
        return pltpu.make_async_remote_copy(
            src_ref=filt_hbm.at[:, pl.ds(pl.multiple_of(grp * span, LANES), span)], dst_ref=other.at[grp],
            send_sem=zs_sem, recv_sem=zr_sem, device_id={"ctx": away + r},
        )

    def filter_across(o, share):
        return pltpu.make_async_remote_copy(
            src_ref=other.at[share], dst_ref=other.at[share], send_sem=xs_sem.at[o], recv_sem=xr_sem.at[o],
            device_id={"grp": lax.rem(grp + o, parts)},
        )

    pl.semaphore_wait(barrier, n - 1 + parts - 1)
    filter_over().start()
    turn(1)
    halo_start((1,))
    turn(2)
    halo_start((2,))
    for i in (4, 5, 6):
        loads[i].start()
    loads[3].wait()
    for ref, shift in ((taps.at[0], low), (alt, cpad - cblk - low)):
        for b, (first, row) in enumerate(pieces):
            base = first - shift + row
            lo, hi = max(base, 0), min(base + rows, channels)
            at = b * rows + lo - base
            ref[:, 0:TAPS, at : at + hi - lo] = tin[:, :, lo:hi]
    turner = unit(True).astype(F32)
    for g in range(groups):
        source = alt[:, :, cp - (g + 1) * LANES : cp - g * LANES].reshape(24, LANES)
        taps[1, :, :, g * LANES : (g + 1) * LANES] = jnp.dot(
            source, turner, precision=lax.Precision.HIGHEST, preferred_element_type=F32
        ).reshape(3, 8, LANES)

    def product(g, row, count, way):
        ls = slice(g * LANES, (g + 1) * LANES)
        prod[way, row : row + count, ls] = short_sum(xs, taps, way, 1, ls, row, count) * short_sum(
            xs, taps, way, 2, ls, row, count
        )

    for g in [*range(groups // 2, groups), *range(groups // 2)]:
        product(g, 8, LANES - 8, 0)
        product(g, 0, LANES - 8, 1)

    turn(0)
    halo_start((0,))
    def rel(m):
        return lax.rem(m + side * own, nch)

    first, second = side, 1 - side

    def near_copy(m, j):
        return pltpu.make_async_remote_copy(
            src_ref=snd.at[m, j], dst_ref=near.at[m, slot],
            send_sem=s_sem.at[m], recv_sem=r_sem.at[m], device_id={"ctx": home + j},
        )

    def far_copy(i, j):
        return pltpu.make_async_remote_copy(
            src_ref=snd.at[own + i, j, 0], dst_ref=far.at[i, slot],
            send_sem=fs_sem.at[i], recv_sem=fr_sem.at[i], device_id={"ctx": away + j},
        )

    def place_of(j):
        return jnp.where(side == 0, j, half - 1 - j)

    def back_copy(m, j):
        return pltpu.make_async_remote_copy(
            src_ref=osnd.at[m, place_of(j)], dst_ref=orcv.at[m, r],
            send_sem=os_sem.at[m], recv_sem=or_sem.at[m], device_id={"ctx": home + j},
        )

    def part_copy(i, j):
        return pltpu.make_async_remote_copy(
            src_ref=psnd.at[i, place_of(j)], dst_ref=prcv.at[i, r],
            send_sem=ps_sem.at[i], recv_sem=pr_sem.at[i], device_id={"ctx": away + j},
        )

    def all_of(src, dst, send_sem, recv_sem):
        return pltpu.make_async_remote_copy(
            src_ref=src, dst_ref=dst, send_sem=send_sem, recv_sem=recv_sem,
            device_id={"ctx": lax.rem(me + 1, n)},
        )

    def all_near(m):
        some = pl.ds(0, half - 1)
        return all_of(snd.at[m, some], near.at[m, some], s_sem.at[m], r_sem.at[m])

    def all_far(i):
        return all_of(far.at[i], far.at[i], fs_sem.at[i], fr_sem.at[i])

    def all_part(i):
        return all_of(psnd.at[i], prcv.at[i], ps_sem.at[i], pr_sem.at[i])

    def all_back(m):
        some = pl.ds(0, half - 1)
        return all_of(osnd.at[m, some], orcv.at[m, some], os_sem.at[m], or_sem.at[m])

    def each(first, act):
        def step(o, carry):
            act(lax.rem(r + o, half))
            return carry

        lax.fori_loop(first, half, step, 0, unroll=True if half <= 8 else 1)

    halo_wait((1, 2))
    for i in range(own):
        for m in (i, own + i):
            for g in range(m * per_chunk, (m + 1) * per_chunk):
                ls = slice(g * LANES, (g + 1) * LANES)
                product(g, 0, 8, 0)
                product(g, LANES - 8, 8, 1)
                pa = to_channel_major(prod[0, :, ls].astype(BF16), eye).astype(BF16)
                pb = to_channel_major(prod[1, :, ls].astype(BF16), flip).astype(BF16)
                at = (g - m * per_chunk) * dests
                for s in range(dests):
                    piece = slice(s * rows, (s + 1) * rows)
                    snd[rel(m), at + s, first] = pa[piece]
                    snd[rel(m + own), half - 1 - at - s, second] = pb[piece]
        each(1, lambda j: near_copy(i, j).start())
    for i in range(own):
        each(0, lambda j: far_copy(i, j).start())
    for i in range(own):
        each(1, lambda j: near_copy(own + i, j).start())

    halo_wait((0,))
    for g in range(groups):
        ls = slice(g * LANES, (g + 1) * LANES)
        for way in range(2):
            q = short_sum(xs, taps, way, 0, ls, 0, LANES)
            high = q.astype(BF16)
            rest = (q - high.astype(F32)).astype(BF16)
            qmix[way, ls, :] = to_channel_major(high, eye) + to_channel_major(rest, eye)

    for i in (4, 5, 6):
        loads[i].wait()
    row = lax.broadcasted_iota(jnp.int32, (cpad, cblk), 0)
    col = lax.broadcasted_iota(jnp.int32, (cpad, cblk), 1)
    places = [
        (row == jnp.where(side == of, low + col, low + cblk - 1 - col)).astype(F32).astype(BF16) for of in range(2)
    ]

    def spectra(dst, shares):
        for which, place in enumerate(places):
            lag = [jnp.zeros((cpad, LANES), BF16)]
            for share in shares:
                padded = mm(place, share).astype(BF16)
                lag += [padded[:, at : at + LANES] for at in range(0, share.shape[-1], LANES)]
            for d in range(len(lag) - 1):
                line = jnp.concatenate([lag[d], lag[d + 1]], axis=1)
                dst[which, d] = mm(line, fwd[0]) + mm(line, fwd[1])

    spectra(hown, [filt[...]])
    filter_over().wait_recv()
    for o in range(1, parts):
        filter_across(o, grp).start()

    re, im = slice(0, LANES), slice(LANES, 2 * LANES)

    def pair(ref, *index):
        return ref[(*index, re)], ref[(*index, im)]

    def times(x, h):
        return x[0] * h[0] - x[1] * h[1], x[0] * h[1] + x[1] * h[0]

    def block_sums(spec, kind, top, out_at, x_at, at, back=None, more=None):
        rs = pl.ds(at, 8)
        hs = pl.ds(top + at, 8)
        ahead, behind = (x_at, back) if more is None else (None, x_at)
        if half > 8:
            def output(t, carry):
                def term(seq, shift, d, total):
                    y = times(pair(xh, *seq, t + shift - d, rs), pair(spec, kind, d, hs))
                    return total[0] + y[0], total[1] + y[1]

                total = (jnp.zeros((8, LANES), F32),) * 2
                if ahead is not None:
                    total = lax.fori_loop(0, t + 1, functools.partial(term, ahead, 0), total)
                if behind is not None:
                    total = lax.fori_loop(t + 1, t + half + 1, functools.partial(term, behind, half), total)
                yh[out_at, t, rs, re], yh[out_at, t, rs, im] = total
                return carry

            lax.fori_loop(0, half, output, 0)
            return
        x = {}
        if behind is not None:
            x.update({t: pair(xh, *behind, t, rs) for t in range(half)})
        if ahead is not None:
            x.update({half + t: pair(xh, *ahead, t, rs) for t in range(half)})
        tile = 4
        for t0 in range(half, 2 * half, tile):
            acc = [None] * tile
            for d in range(2 * half):
                used = [u for u in range(tile) if t0 + u - d in x]
                if not used:
                    continue
                h = pair(spec, kind, d, hs)
                for u in used:
                    y = times(x[t0 + u - d], h)
                    acc[u] = y if acc[u] is None else (acc[u][0] + y[0], acc[u][1] + y[1])
            for u in range(tile):
                t = t0 - half + u
                yh[out_at, t, rs, re], yh[out_at, t, rs, im] = acc[u]

    def transform(dst, blocks):
        x = jnp.concatenate(blocks, axis=0)
        spec = mm(x, fwd[0, 0:LANES, :]) + mm(x, fwd[1, 0:LANES, :])
        xh[dst] = spec.reshape(half, rows, 2 * LANES)

    def result(which):
        y = yh[which].reshape(half * rows, 2 * LANES)
        high = y.astype(BF16)
        rest = (y - high.astype(F32)).astype(BF16)
        way = first if which == 0 else second
        both = mm(high, inv[way])
        y = (both[:, :LANES] + both[:, LANES:] + mm(rest, inv[way, :, 0:LANES])).astype(BF16)
        return [y[t * rows : (t + 1) * rows] for t in range(half)]

    def octets(body):
        def step(i, carry):
            body(pl.multiple_of(i * 8, 8))
            return carry

        lax.fori_loop(0, rows // 8, step, 0)

    def receive(m):
        all_near(m).wait_recv()
        near[m, slot] = snd[m, r]

    def send_back(m):
        for t, y in enumerate(result(0)):
            osnd[m, t, 0] = y
        for t, y in enumerate(result(1)):
            osnd[m, half - 1 - t, 1] = y
        each(1, lambda j: back_copy(m, j).start())
        orcv[m, r] = osnd[m, slot]

    def mix(m):
        for g in range(m * per_chunk, (m + 1) * per_chunk):
            ls = slice(g * LANES, (g + 1) * LANES)
            at = [(g - m * per_chunk) * dests + s for s in range(dests)]
            a = jnp.concatenate([orcv[rel(m), d, first] for d in at], axis=0).astype(F32)
            b = jnp.concatenate([orcv[rel(m + own), half - 1 - d, second] for d in at], axis=0).astype(F32)
            if m < own:
                rest = [prcv[m, jnp.where(side == 1, d, half - 1 - d)] for d in at]
                rest = jnp.concatenate(rest, axis=0).astype(F32)
                a, b = jnp.where(side == 1, a + rest, a), jnp.where(side == 1, b, b + rest)
            mixed = qmix[0, ls, :] * a + qmix[1, ls, :] * b
            for s, (start, row) in enumerate(pieces[g * dests : (g + 1) * dests]):
                lo, hi = max(row, low), min(row + rows, low + cblk)
                to = 8 + start - low
                xf[0, to + lo : to + hi, :] = mixed[s * rows + lo - row : s * rows + hi - row]

    for i in range(own):
        m = i
        receive(m)
        transform((i, 0), [near[m, t, 0] for t in range(half)])
        octets(lambda at: block_sums(hown, 0, m * rows, 0, (i, 0), at, more=True))
        for t, y in enumerate(result(0)):
            psnd[m, t] = y
        each(0, lambda j: part_copy(m, j).start())
    for i in range(own):
        m = i
        transform((i, 1), [near[m, half - 1 - t, 1] for t in range(half)])
        all_far(m).wait_recv()
        transform((i, 2), [far[m, t] for t in range(half)])

        def both(at):
            block_sums(hown, 0, m * rows, 0, (i, 0), at)
            block_sums(hown, 1, m * rows, 1, (i, 1), at, back=(i, 2))

        octets(both)
        send_back(m)
    for o in range(1, parts):
        filter_across(o, lax.rem(grp + parts - o, parts)).wait_recv()
    spectra(hother, [other[g] for g in range(parts)])
    for i in range(own):
        m = i
        receive(own + m)
        transform((0, 0), [near[own + m, t, 0] for t in range(half)])
        transform((0, 1), [near[own + m, half - 1 - t, 1] for t in range(half)])

        def both(at):
            block_sums(hother, 0, m * rows, 0, (0, 0), at)
            block_sums(hother, 1, m * rows, 1, (0, 1), at)

        octets(both)
        send_back(own + m)
    for i in range(own):
        all_back(i).wait_recv()
    for i in range(own):
        all_back(own + i).wait_recv()
        mix(own + i)
        all_part(i).wait_recv()
        mix(i)
    out[...] = xf[0, 8:held, :].astype(BF16)

    for m in range(nch):
        all_near(m).wait_send()
        all_back(m).wait_send()
    for i in range(own):
        all_far(i).wait_send()
        all_part(i).wait_send()
    filter_over().wait_send()
    for o in range(1, parts):
        filter_across(o, grp).wait_send()

    @pl.when(me < n - 1)
    def _():
        for a in range(3):
            halo(a, True).wait_send()

    @pl.when(me > 0)
    def _():
        for a in range(3):
            halo(a, False).wait_send()


def hand_on(src, dst, held, in_sem, out_sem):
    size = src.shape[0] // SHARES
    rows = [pl.ds(i * size, size) for i in range(SHARES)]
    into = [pltpu.make_async_copy(src.at[r], held.at[r], in_sem.at[i]) for i, r in enumerate(rows)]
    away = [pltpu.make_async_copy(held.at[r], dst.at[r], out_sem.at[i]) for i, r in enumerate(rows)]
    for copy in into:
        copy.start()
    for one, other in zip(into, away):
        one.wait()
        other.start()
    for copy in away:
        copy.wait()


def on_device(queries, key_rows, value_rows, short_taps, long_filter):
    n = lax.axis_size("ctx")
    parts = lax.axis_size("grp")
    channels, tokens = queries.shape
    cblk, length = long_filter.shape
    cpad, low, rows = dims_of(cblk)
    half = n // 2
    nch = 2 * cpad // rows
    own = nch // 2
    cp = n * cpad
    taps = jnp.swapaxes(short_taps, 1, 2)
    hbm = pl.BlockSpec(memory_space=pltpu.MemorySpace.HBM)
    vmem = pl.BlockSpec(memory_space=pltpu.VMEM)
    dma = pltpu.SemaphoreType.DMA
    mixed = pl.pallas_call(
        functools.partial(kernel, n, parts, cblk),
        out_shape=jax.ShapeDtypeStruct((channels, tokens), BF16),
        in_specs=[hbm] * 7,
        out_specs=vmem,
        scratch_shapes=[
            pltpu.VMEM((3, channels, tokens), BF16),
            pltpu.VMEM((3, TAPS, channels), F32),
            pltpu.VMEM((cblk, length), BF16),
            pltpu.VMEM((parts, cblk, half * LANES // parts), BF16),
            dma((7,)),
            pltpu.VMEM((3, 8, cp), F32),
            pltpu.VMEM((2, 3, 8, cp), F32),
            pltpu.VMEM((3, channels + 24, LANES), F32),
            pltpu.VMEM((3, LANES + 16, cp), F32),
            pltpu.VMEM((2, cp, LANES), F32),
            pltpu.VMEM((2, LANES, cp), F32),
            pltpu.VMEM((nch, half, 2, rows, LANES), BF16),
            pltpu.VMEM((nch, half, 2, rows, LANES), BF16),
            pltpu.VMEM((own, half, rows, LANES), BF16),
            pltpu.VMEM((nch, half, 2, rows, LANES), BF16),
            pltpu.VMEM((nch, half, 2, rows, LANES), BF16),
            pltpu.VMEM((own, half, rows, LANES), BF16),
            pltpu.VMEM((own, half, rows, LANES), BF16),
            pltpu.VMEM((2, 2 * LANES, 2 * LANES), BF16),
            pltpu.VMEM((2, 2 * LANES, 2 * LANES), BF16),
            pltpu.VMEM((2, n, cpad, 2 * LANES), F32),
            pltpu.VMEM((2, half, cpad, 2 * LANES), F32),
            pltpu.VMEM((own, 3, half, rows, 2 * LANES), F32),
            pltpu.VMEM((2, half, rows, 2 * LANES), F32),
            dma((2, 3)),
            dma((2, 3)),
            dma((nch,)),
            dma((nch,)),
            dma((own,)),
            dma((own,)),
            dma((nch,)),
            dma((nch,)),
            dma((own,)),
            dma((own,)),
            dma(()),
            dma(()),
            dma((parts,)),
            dma((parts,)),
        ],
        compiler_params=pltpu.CompilerParams(
            collective_id=0, has_side_effects=True, vmem_limit_bytes=62 * 1024 * 1024
        ),
    )(queries, key_rows, value_rows, taps, long_filter, *(jnp.asarray(x) for x in dft_tables()))
    return pl.pallas_call(
        hand_on,
        out_shape=jax.ShapeDtypeStruct((channels, tokens), BF16),
        in_specs=[hbm],
        out_specs=hbm,
        scratch_shapes=[pltpu.VMEM((channels, tokens), BF16), dma((SHARES,)), dma((SHARES,))],
    )(mixed)


def solution(mesh):
    placed = (
        P(None, ("grp", "ctx")),
        P(None, ("grp", "ctx")),
        P(None, ("grp", "ctx")),
        P(),
        P("ctx", None),
    )
    return jax.shard_map(
        on_device, mesh=mesh, in_specs=placed, out_specs=P(None, ("grp", "ctx")), check_vma=False
    )
```
